512 devices in a mesh: brick: 32 (over z_hi, y), stack: 16 (over x, z_lo, core).
Axes of the slice: x: 4, y: 8, z: 8 (z_hi: 4, z_lo: 2; z = z_hi * 2 + z_lo), core: 2. Of those that a mesh axis runs over, the one named last changes fastest.
Arguments:
- estimate: float32 [256, 1024, 128], P('stack', 'brick'), may hold values from 0.5 to 2
- view_data: float32 [6, 256, 1024, 128], P(None, 'stack', 'brick'), may hold values from 0.25 to 4
- psf_taps: float32 [6, 3, 31], replicated, may hold values from 0.05 to 1
- offsets: int32 [6], replicated, may hold values from 0 to 31, as said below
- coverage: int32 [6, 32], P(None, 'brick'), may hold values from 0 to 1, as said below
Outputs:
- updated: float32 [256, 1024, 128], P('stack', 'brick')
The draws below stay inside these ranges and needn't reach their ends.
Inputs may be any that keep to these rules, and one draw needn't show every extreme that they name: Tile j of view v images brick (j + offsets[v]) mod 32. `coverage`: every brick is covered by at least one view.
All inputs are finite; a program needn't handle non-finite values.
Results may differ from the reference program's by a relative error of at most 0.0001.
Values sent between devices are 32-bit elements; how exact they have to be, the bound alone decides.
No kernel may reach another device: no remote copies, remote signals or barrier semaphores. Data moves between devices by JAX's collectives and lax.ppermute only.
A program may use at most 128 MiB of HBM per device.

```python
import math
import jax
import jax.numpy as jnp
from jax import lax

V = 6
TAPS = 31
HALF = 15
X = 128
CY = 32
NZ = 256
NY = 1024
TILES = 32


def draw_offsets(key, part):
    first_key = jax.random.fold_in(key, 11)
    second_key = jax.random.fold_in(key, 12)
    values = jax.random.randint(first_key, (V,), 0, TILES)
    view_order = jax.random.permutation(second_key, V)
    bit_count = (TILES - 1).bit_length()
    for bit_index in range(bit_count):
        target = view_order[bit_index]
        values = values.at[target].set(jnp.bitwise_or(values[target], 1 << bit_index))
    values = values.at[view_order[bit_count]].set(TILES - 1)
    return values.astype(jnp.int32)


def draw_coverage(key, part):
    first_key = jax.random.fold_in(key, 21)
    second_key = jax.random.fold_in(key, 22)
    chance = jax.random.randint(first_key, (V, TILES), 0, 100)
    forced = jax.random.randint(second_key, (TILES,), 0, V)
    picked = jnp.arange(V)[:, None] == forced[None, :]
    return jnp.logical_or(chance < 55, picked).astype(jnp.int32)


def steps_of(key, shape, cuts, low, high):
    factor_of, own = 1.0, jax.random.fold_in(key, 6)
    for position, blocks in cuts:
        heights = jnp.exp(jax.random.uniform(jax.random.fold_in(own, position), (blocks,), jnp.float32, low / len(cuts), high / len(cuts)))
        factor_of = factor_of * jnp.repeat(heights, shape[position] // blocks).reshape([-1 if axis == position else 1 for axis in range(len(shape))])
    return factor_of


def setup_inputs(seed: int = 0) -> dict:
    key_of = jax.random.split(jax.random.key(seed), 6)
    estimate = jnp.clip(0.5 + 1.5 * jax.random.uniform(key_of[0], (NZ, NY, X), jnp.float32) ** steps_of(key_of[0], (NZ, NY, X), ((0, 16), (1, 32)), -0.2, 0.2), 0.5, 2.0)
    view_data = jnp.clip(jnp.exp(math.log(4.0) - 2.7725887 * jax.random.uniform(key_of[1], (V, NZ, NY, X), jnp.float32) ** steps_of(key_of[1], (V, NZ, NY, X), ((1, 16), (2, 32)), -0.2, 0.2)), 0.25, 4.0)
    psf_taps = jnp.clip(jnp.exp(jax.random.uniform(key_of[2], (V, 3, TAPS), jnp.float32, math.log(0.05), math.log(1.0))), 0.05, 1.0)
    offsets = draw_offsets(jax.random.fold_in(key_of[5], 71), 0)
    coverage = draw_coverage(jax.random.fold_in(key_of[5], 71), 0)
    return dict(estimate=estimate, view_data=view_data, psf_taps=psf_taps, offsets=offsets, coverage=coverage)


def band_matrix(taps, out_count, in_count, lead):
    out_index = jnp.arange(out_count)[:, None]
    in_index = jnp.arange(in_count)[None, :]
    distance = in_index - out_index + lead
    matrix = jnp.zeros((out_count, in_count), jnp.float32)
    for tap_index in range(TAPS):
        matrix = matrix + jnp.where(distance == tap_index, taps[tap_index], jnp.float32(0.0))
    return matrix


def along_first(matrix, field):
    return jnp.einsum("ij,jyx->iyx", matrix, field, precision=lax.Precision.HIGHEST)


def along_second(matrix, field):
    return jnp.einsum("ij,zjx->zix", matrix, field, precision=lax.Precision.HIGHEST)


def along_third(matrix, field):
    return jnp.einsum("ij,zyj->zyi", matrix, field, precision=lax.Precision.HIGHEST)


def reference(estimate, view_data, psf_taps, offsets, coverage):
    kernels = psf_taps / jnp.sum(psf_taps, axis=-1, keepdims=True)
    flipped = kernels[..., ::-1]
    cover_count = jnp.repeat(jnp.sum(coverage, axis=0), CY).astype(jnp.float32)
    summed = jnp.zeros_like(estimate)
    for view_index in range(V):
        blurred = along_first(band_matrix(kernels[view_index, 0], NZ, NZ, HALF), estimate)
        blurred = along_second(band_matrix(kernels[view_index, 1], NY, NY, HALF), blurred)
        blurred = along_third(band_matrix(kernels[view_index, 2], X, X, HALF), blurred)
        recorded = view_data[view_index].astype(jnp.float32)
        doubled = jnp.concatenate([recorded, recorded], axis=1)
        start_row = (NY - offsets[view_index] * CY).astype(jnp.int32)
        owned_data = lax.dynamic_slice_in_dim(doubled, start_row, NY, axis=1)
        cover_mask = jnp.repeat(coverage[view_index], CY).astype(jnp.float32)
        ratio_field = cover_mask[None, :, None] * owned_data / blurred
        back_field = along_third(band_matrix(flipped[view_index, 2], X, X, HALF), ratio_field)
        back_field = along_second(band_matrix(flipped[view_index, 1], NY, NY, HALF), back_field)
        back_field = along_first(band_matrix(flipped[view_index, 0], NZ, NZ, HALF), back_field)
        summed = summed + back_field
    return estimate * summed / cover_count[None, :, None]
```

```python
import functools

import jax
import jax.numpy as jnp
from jax import lax
from jax.experimental import pallas as pl
from jax.experimental.pallas import tpu as pltpu
from jax.sharding import PartitionSpec as P

F32, BF16 = jnp.float32, jnp.bfloat16


def split(values):
    high = values.astype(BF16)
    return high, (values - high.astype(F32)).astype(BF16)


def split_outside(values):
    high = lax.reduce_precision(values, 8, 7)
    return high.astype(BF16), (values - high).astype(BF16)


def dot(left, right):
    return jnp.dot(left, right, preferred_element_type=F32)


def band(taps, rows, columns, lead):
    count = taps.shape[1]
    tap = jnp.arange(columns)[None, :] - jnp.arange(rows)[:, None] + lead
    chosen = jnp.arange(count)[None, None, :] == tap[:, :, None]
    return jnp.sum(jnp.where(chosen[None], taps[:, None, None, :], 0.0), axis=-1)


def forward_kernel(half, taps_ref, low_ref, mid_ref, high_ref, lateral_ref, across_ref, out_ref, wide_ref):
    views, depth, rows, width = out_ref.shape
    refs = (low_ref, mid_ref, high_ref)
    for part in range(3):

        def lateral(pair, carry, part=part):
            z = pair * 2
            first_h, first_l = split(refs[part][z])
            second_h, second_l = split(refs[part][z + 1])
            upper = jnp.concatenate([first_h, second_h], axis=1)
            lower = jnp.concatenate([first_l, second_l], axis=1)
            stacked = jnp.concatenate([upper, lower, upper], axis=0)
            result = dot(lateral_ref[...], stacked)
            wide_ref[part * depth + z] = result[:, :width]
            wide_ref[part * depth + z + 1] = result[:, width:]
            return carry

        lax.fori_loop(0, depth // 2, lateral, 0)

    taps = taps_ref.shape[1]
    start = depth - half
    groups = rows // 8

    def axial(step, carry):
        view, group = step // groups, step % groups
        at = pl.ds(pl.multiple_of(view * rows + group * 8, 8), 8)
        field = [wide_ref[z, at, :] for z in range(start, start + depth + taps - 1)]
        for z in range(depth):
            total = taps_ref[view, 0] * field[z]
            for t in range(1, taps):
                total += taps_ref[view, t] * field[z + t]
            out_ref[view, z, pl.ds(pl.multiple_of(group * 8, 8), 8), :] = total
        return carry

    lax.fori_loop(0, views * groups, axial, 0)

    def across(view, carry):
        field = out_ref[view].reshape(depth * rows, width)
        upper, lower = split(field)
        both = dot(jnp.concatenate([upper, lower], axis=1), across_ref[view])
        out_ref[view] = (both[:, :width] + both[:, width:]).reshape(depth, rows, width)
        return carry

    lax.fori_loop(0, views, across, 0)


def back_kernel(half, taps_ref, cover_ref, tiles_ref, blurred_ref, across_ref, lateral_ref, low_ref, mid_ref, high_ref, near_ref, wide_ref):
    views, depth, rows, width = blurred_ref.shape
    halves = tiles_ref.shape[1]

    def across(view, carry):
        owned = jnp.concatenate([tiles_ref[:, part, view] for part in range(halves)], axis=1)
        ratio = (cover_ref[view].astype(F32) * owned / blurred_ref[view]).reshape(depth * rows, width)
        upper, lower = split(ratio)
        both = dot(jnp.concatenate([upper, lower], axis=1), across_ref[view])
        near_ref[view] = (both[:, :width] + both[:, width:]).reshape(depth, rows, width)
        return carry

    lax.fori_loop(0, views, across, 0)

    taps = taps_ref.shape[1]
    start = depth - half
    groups = rows // 8

    def axial(step, carry):
        view, group = step // groups, step % groups
        at = pl.ds(pl.multiple_of(group * 8, 8), 8)
        into = pl.ds(pl.multiple_of(view * rows + group * 8, 8), 8)
        field = [near_ref[view, z, at, :] for z in range(depth)]
        for z in range(3 * depth):
            total = None
            for source in range(depth):
                t = z - start - source
                if 0 <= t < taps:
                    term = taps_ref[view, t] * field[source]
                    total = term if total is None else total + term
            wide_ref[z, into, :] = jnp.zeros((8, width), F32) if total is None else total
        return carry

    lax.fori_loop(0, views * groups, axial, 0)

    outs = (low_ref, mid_ref, high_ref)
    for part in range(3):

        def lateral(pair, carry, part=part):
            z = part * depth + pair * 2
            first_h, first_l = split(wide_ref[z])
            second_h, second_l = split(wide_ref[z + 1])
            upper = jnp.concatenate([first_h, second_h], axis=1)
            lower = jnp.concatenate([first_l, second_l], axis=1)
            result = dot(lateral_ref[0], upper) + dot(lateral_ref[0], lower) + dot(lateral_ref[1], upper)
            outs[part][pair * 2] = result[:, :width]
            outs[part][pair * 2 + 1] = result[:, width:]
            return carry

        lax.fori_loop(0, depth // 2, lateral, 0)


def turn_kernel(ring, offsets_ref, in_ref, out_ref):
    views = in_ref.shape[1]

    def body(place, carry):
        for view in range(views):
            source = lax.rem(place + ring - lax.rem(offsets_ref[view], ring), ring)
            out_ref[place, view] = in_ref[source, view]
        return carry

    lax.fori_loop(0, ring, body, 0)


SMEM = pl.BlockSpec(memory_space=pltpu.SMEM)
VMEM = pl.BlockSpec(memory_space=pltpu.VMEM)
PARAMS = pltpu.CompilerParams(vmem_limit_bytes=48 << 20)


def shards(estimate, view_data, psf_taps, offsets, coverage):
    depth, rows, width = estimate.shape
    views = view_data.shape[0]
    half = (psf_taps.shape[2] - 1) // 2
    reach = half + 1
    ring = lax.axis_size("brick")
    stacks = lax.axis_size("stack")
    up = [(i, i + 1) for i in range(stacks - 1)]
    down = [(i + 1, i) for i in range(stacks - 1)]
    right = [(i, i + 1) for i in range(ring - 1)]
    left = [(i + 1, i) for i in range(ring - 1)]

    parts = ring // depth
    strip = rows // parts
    pieces = view_data.reshape(views, ring, strip, width).transpose(1, 0, 2, 3)
    spread = lax.all_to_all(pieces, "brick", 0, 0, tiled=True)

    head = lax.ppermute(estimate[:, rows - reach :], "brick", right)
    tail = lax.ppermute(estimate[:, :reach], "brick", left)
    mid = jnp.concatenate([head, estimate, tail], axis=1)
    low = lax.ppermute(mid, "stack", up)
    high = lax.ppermute(mid, "stack", down)

    kernels = psf_taps / jnp.sum(psf_taps, axis=-1, keepdims=True)
    flipped = kernels[..., ::-1]
    wide = rows + 2 * reach
    lateral = band(kernels[:, 1], rows, wide, half - reach)
    lateral_h, lateral_l = split_outside(lateral.reshape(views * rows, wide))
    lateral_on = jnp.concatenate([lateral_h, lateral_h, lateral_l], axis=1)
    lateral_back = lateral.transpose(2, 0, 1).reshape(wide, views * rows)
    lateral_back = jnp.stack(split_outside(lateral_back))

    def across_of(taps):
        high_part, low_part = split_outside(band(taps, width, width, half).transpose(0, 2, 1))
        top = jnp.concatenate([high_part, low_part], axis=2)
        return jnp.concatenate([top, jnp.concatenate([high_part, jnp.zeros_like(low_part)], axis=2)], axis=1)

    across_on, across_back = across_of(kernels[:, 2]), across_of(flipped[:, 2])

    blurred = pl.pallas_call(
        functools.partial(forward_kernel, half),
        out_shape=jax.ShapeDtypeStruct((views, depth, rows, width), F32),
        in_specs=[SMEM, VMEM, VMEM, VMEM, VMEM, VMEM],
        out_specs=VMEM,
        scratch_shapes=[pltpu.VMEM((3 * depth, views * rows, width), F32)],
        compiler_params=PARAMS,
        name="forward",
    )(kernels[:, 0], low, mid, high, lateral_on, across_on)

    turned = pl.pallas_call(
        functools.partial(turn_kernel, ring),
        out_shape=jax.ShapeDtypeStruct(spread.shape, F32),
        in_specs=[SMEM, VMEM],
        out_specs=VMEM,
        compiler_params=PARAMS,
        name="turn",
    )(offsets, spread)
    tiles = lax.all_to_all(turned, "brick", 0, 0, tiled=True)
    tiles = tiles.reshape(depth, parts, views, strip, width)

    slab = jax.ShapeDtypeStruct((depth, wide, width), F32)
    below, own, above = pl.pallas_call(
        functools.partial(back_kernel, half),
        out_shape=(slab, slab, slab),
        in_specs=[SMEM, SMEM, VMEM, VMEM, VMEM, VMEM],
        out_specs=(VMEM, VMEM, VMEM),
        scratch_shapes=[
            pltpu.VMEM((views, depth, rows, width), F32),
            pltpu.VMEM((3 * depth, views * rows, width), F32),
        ],
        compiler_params=PARAMS,
        name="back",
    )(kernels[:, 0], coverage[:, 0], tiles, blurred, across_back, lateral_back)

    total = own + lax.ppermute(below, "stack", down) + lax.ppermute(above, "stack", up)
    from_right = lax.ppermute(total[:, :reach], "brick", left)
    from_left = lax.ppermute(total[:, rows + reach :], "brick", right)
    summed = total[:, reach : rows + reach]
    gap = jnp.zeros((depth, rows - reach, width), F32)
    summed = summed + jnp.concatenate([from_left, gap], axis=1) + jnp.concatenate([gap, from_right], axis=1)
    cover_count = jnp.sum(coverage[:, 0].astype(F32))
    return estimate * summed / cover_count


def solution(mesh):
    placed = (
        P("stack", "brick", None),
        P(None, "stack", "brick", None),
        P(),
        P(),
        P(None, "brick"),
    )
    return jax.shard_map(
        shards, mesh=mesh, in_specs=placed, out_specs=P("stack", "brick", None), check_vma=False
    )
```

```python
import functools

import jax
import jax.numpy as jnp
from jax import lax
from jax.experimental import pallas as pl
from jax.experimental.pallas import tpu as pltpu
from jax.sharding import PartitionSpec as P

F32, BF16 = jnp.float32, jnp.bfloat16
ROW = 8
DIRECT = 3


def split(values):
    high = values.astype(BF16)
    return high, (values - high.astype(F32)).astype(BF16)


def split_outside(values):
    high = lax.reduce_precision(values, 8, 7)
    return high.astype(BF16), (values - high).astype(BF16)


def dot(left, right):
    return jnp.dot(left, right, preferred_element_type=F32)


def band(taps, rows, columns, lead):
    count = taps.shape[1]
    tap = jnp.arange(columns)[None, :] - jnp.arange(rows)[:, None] + lead
    chosen = jnp.arange(count)[None, None, :] == tap[:, :, None]
    return jnp.sum(jnp.where(chosen[None], taps[:, None, None, :], 0.0), axis=-1)


def forward_kernel(half, taps_ref, low_ref, mid_ref, high_ref, lateral_ref, across_ref, out_ref, wide_ref):
    views, depth, rows, width = out_ref.shape
    refs = (low_ref, mid_ref, high_ref)
    for part in range(3):

        def lateral(pair, carry, part=part):
            z = pair * 2
            first_h, first_l = split(refs[part][z])
            second_h, second_l = split(refs[part][z + 1])
            upper = jnp.concatenate([first_h, second_h], axis=1)
            lower = jnp.concatenate([first_l, second_l], axis=1)
            stacked = jnp.concatenate([upper, lower, upper], axis=0)
            result = dot(lateral_ref[...], stacked)
            wide_ref[part * depth + z] = result[:, :width]
            wide_ref[part * depth + z + 1] = result[:, width:]
            return carry

        lax.fori_loop(0, depth // 2, lateral, 0)

    taps = taps_ref.shape[1]
    start = depth - half
    groups = rows // 8

    def axial(step, carry):
        view, group = step // groups, step % groups
        at = pl.ds(pl.multiple_of(view * rows + group * 8, 8), 8)
        field = [wide_ref[z, at, :] for z in range(start, start + depth + taps - 1)]
        for z in range(depth):
            total = taps_ref[view, 0] * field[z]
            for t in range(1, taps):
                total += taps_ref[view, t] * field[z + t]
            out_ref[view, z, pl.ds(pl.multiple_of(group * 8, 8), 8), :] = total
        return carry

    lax.fori_loop(0, views * groups, axial, 0)

    def across(view, carry):
        field = out_ref[view].reshape(depth * rows, width)
        upper, lower = split(field)
        both = dot(jnp.concatenate([upper, lower], axis=1), across_ref[view])
        out_ref[view] = (both[:, :width] + both[:, width:]).reshape(depth, rows, width)
        return carry

    lax.fori_loop(0, views, across, 0)


def back_kernel(half, taps_ref, cover_ref, order_ref, *refs):
    tiles_ref, *direct = refs[:-8]
    blurred_ref, across_ref, lateral_ref, low_ref, mid_ref, high_ref, near_ref, wide_ref = refs[-8:]
    views, depth, rows, width = blurred_ref.shape
    halves, spread = tiles_ref.shape[1:3]

    def across(slot, owned):
        view = order_ref[slot]
        ratio = (cover_ref[view].astype(F32) * owned / blurred_ref[view]).reshape(depth * rows, width)
        upper, lower = split(ratio)
        both = dot(jnp.concatenate([upper, lower], axis=1), across_ref[view])
        near_ref[view] = (both[:, :width] + both[:, width:]).reshape(depth, rows, width)

    for slot in range(views):
        if slot < spread:
            across(slot, jnp.concatenate([tiles_ref[:, part, slot] for part in range(halves)], axis=1))
        else:
            across(slot, direct[slot - spread][...])

    taps = taps_ref.shape[1]
    start = depth - half
    groups = rows // 8

    def axial(step, carry):
        view, group = step // groups, step % groups
        at = pl.ds(pl.multiple_of(group * 8, 8), 8)
        into = pl.ds(pl.multiple_of(view * rows + group * 8, 8), 8)
        field = [near_ref[view, z, at, :] for z in range(depth)]
        for z in range(3 * depth):
            total = None
            for source in range(depth):
                t = z - start - source
                if 0 <= t < taps:
                    term = taps_ref[view, t] * field[source]
                    total = term if total is None else total + term
            wide_ref[z, into, :] = jnp.zeros((8, width), F32) if total is None else total
        return carry

    lax.fori_loop(0, views * groups, axial, 0)

    outs = (low_ref, mid_ref, high_ref)
    for part in range(3):

        def lateral(pair, carry, part=part):
            z = part * depth + pair * 2
            first_h, first_l = split(wide_ref[z])
            second_h, second_l = split(wide_ref[z + 1])
            upper = jnp.concatenate([first_h, second_h], axis=1)
            lower = jnp.concatenate([first_l, second_l], axis=1)
            result = dot(lateral_ref[0], upper) + dot(lateral_ref[0], lower) + dot(lateral_ref[1], upper)
            outs[part][pair * 2] = result[:, :width]
            outs[part][pair * 2 + 1] = result[:, width:]
            return carry

        lax.fori_loop(0, depth // 2, lateral, 0)


def turn_kernel(ring, offsets_ref, in_ref, out_ref):
    views = in_ref.shape[1]

    def body(place, carry):
        for view in range(views):
            source = lax.rem(place + ring - offsets_ref[view], ring)
            out_ref[place, view] = in_ref[source, view]
        return carry

    lax.fori_loop(0, ring, body, 0)


def pick_kernel(row, columns, offsets_ref, in_ref, order_ref, sorted_ref, pieces_ref, *direct):
    views = in_ref.shape[0]
    spread = pieces_ref.shape[1]
    cost, moves = [], []
    for view in range(views):
        move = lax.rem(offsets_ref[view], row * columns)
        across, along = lax.rem(move, row), move // row
        near = 2 * jnp.minimum(along, columns - along)
        far = 2 * jnp.minimum(along + 1, columns - 1 - along)
        far = jnp.where(across > 0, far, 0)
        cost.append(jnp.maximum(jnp.minimum(across, row - across), jnp.maximum(near, far)))
        moves.append(move)
    for view in range(views):
        rank = jnp.int32(0)
        for other in range(views):
            if other != view:
                ahead = cost[other] >= cost[view] if other < view else cost[other] > cost[view]
                rank = rank + ahead.astype(jnp.int32)
        order_ref[rank] = jnp.int32(view)
        sorted_ref[rank] = moves[view]
    for slot in range(views):
        view = order_ref[slot]
        if slot < spread:
            pieces_ref[:, slot] = in_ref[view]
        else:
            direct[slot - spread][...] = in_ref[view].reshape(direct[slot - spread].shape)


SMEM = pl.BlockSpec(memory_space=pltpu.SMEM)
VMEM = pl.BlockSpec(memory_space=pltpu.VMEM)
PARAMS = pltpu.CompilerParams(vmem_limit_bytes=48 << 20)


def shards(estimate, view_data, psf_taps, offsets, coverage):
    depth, rows, width = estimate.shape
    views = view_data.shape[0]
    half = (psf_taps.shape[2] - 1) // 2
    reach = half + 1
    ring = lax.axis_size("brick")
    stacks = lax.axis_size("stack")
    up = [(i, i + 1) for i in range(stacks - 1)]
    down = [(i + 1, i) for i in range(stacks - 1)]
    right = [(i, i + 1) for i in range(ring - 1)]
    left = [(i + 1, i) for i in range(ring - 1)]

    parts = ring // depth
    strip = rows // parts
    tile = jax.ShapeDtypeStruct((depth, rows, width), F32)
    order, moves, pieces, *straight = pl.pallas_call(
        functools.partial(pick_kernel, ROW, ring // ROW),
        out_shape=(
            jax.ShapeDtypeStruct((views,), jnp.int32),
            jax.ShapeDtypeStruct((views,), jnp.int32),
            jax.ShapeDtypeStruct((ring, views - DIRECT, strip, width), F32),
        )
        + (tile,) * DIRECT,
        in_specs=[SMEM, VMEM],
        out_specs=(SMEM, SMEM, VMEM) + (VMEM,) * DIRECT,
        compiler_params=PARAMS,
        name="pick",
    )(offsets, view_data.reshape(views, ring, strip, width))
    spread = lax.all_to_all(pieces, "brick", 0, 0, tiled=True)
    hops = [functools.partial(lax.ppermute, axis_name="brick", perm=[(i, (i + by) % ring) for i in range(ring)]) for by in range(1, ring)]
    hops = [lambda x: x] + hops

    def send(slot, x):
        return lax.switch(moves[views - DIRECT + slot], hops, x)

    sent = [send(0, straight[0])]

    head = lax.ppermute(estimate[:, rows - reach :], "brick", right)
    tail = lax.ppermute(estimate[:, :reach], "brick", left)
    mid = jnp.concatenate([head, estimate, tail], axis=1)
    low = lax.ppermute(mid, "stack", up)
    high = lax.ppermute(mid, "stack", down)

    kernels = psf_taps / jnp.sum(psf_taps, axis=-1, keepdims=True)
    flipped = kernels[..., ::-1]
    wide = rows + 2 * reach
    lateral = band(kernels[:, 1], rows, wide, half - reach)
    lateral_h, lateral_l = split_outside(lateral.reshape(views * rows, wide))
    lateral_on = jnp.concatenate([lateral_h, lateral_h, lateral_l], axis=1)
    lateral_back = lateral.transpose(2, 0, 1).reshape(wide, views * rows)
    lateral_back = jnp.stack(split_outside(lateral_back))

    def across_of(taps):
        high_part, low_part = split_outside(band(taps, width, width, half).transpose(0, 2, 1))
        top = jnp.concatenate([high_part, low_part], axis=2)
        return jnp.concatenate([top, jnp.concatenate([high_part, jnp.zeros_like(low_part)], axis=2)], axis=1)

    across_on, across_back = across_of(kernels[:, 2]), across_of(flipped[:, 2])

    turned = pl.pallas_call(
        functools.partial(turn_kernel, ring),
        out_shape=jax.ShapeDtypeStruct(spread.shape, F32),
        in_specs=[SMEM, VMEM],
        out_specs=VMEM,
        compiler_params=PARAMS,
        name="turn",
    )(moves, spread)
    turned, low, mid, high, *waiting = lax.optimization_barrier((turned, low, mid, high, *straight[1:]))
    tiles = lax.all_to_all(turned, "brick", 0, 0, tiled=True)
    sent += [send(slot + 1, x) for slot, x in enumerate(waiting)]

    blurred = pl.pallas_call(
        functools.partial(forward_kernel, half),
        out_shape=jax.ShapeDtypeStruct((views, depth, rows, width), F32),
        in_specs=[SMEM, VMEM, VMEM, VMEM, VMEM, VMEM],
        out_specs=VMEM,
        scratch_shapes=[pltpu.VMEM((3 * depth, views * rows, width), F32)],
        compiler_params=PARAMS,
        name="forward",
    )(kernels[:, 0], low, mid, high, lateral_on, across_on)

    tiles = tiles.reshape(depth, parts, views - DIRECT, strip, width)

    slab = jax.ShapeDtypeStruct((depth, wide, width), F32)
    below, own, above = pl.pallas_call(
        functools.partial(back_kernel, half),
        out_shape=(slab, slab, slab),
        in_specs=[SMEM, SMEM, SMEM] + [VMEM] * (4 + DIRECT),
        out_specs=(VMEM, VMEM, VMEM),
        scratch_shapes=[
            pltpu.VMEM((views, depth, rows, width), F32),
            pltpu.VMEM((3 * depth, views * rows, width), F32),
        ],
        compiler_params=PARAMS,
        name="back",
    )(kernels[:, 0], coverage[:, 0], order, tiles, *sent, blurred, across_back, lateral_back)

    total = own + lax.ppermute(below, "stack", down) + lax.ppermute(above, "stack", up)
    from_right = lax.ppermute(total[:, :reach], "brick", left)
    from_left = lax.ppermute(total[:, rows + reach :], "brick", right)
    summed = total[:, reach : rows + reach]
    gap = jnp.zeros((depth, rows - reach, width), F32)
    summed = summed + jnp.concatenate([from_left, gap], axis=1) + jnp.concatenate([gap, from_right], axis=1)
    cover_count = jnp.sum(coverage[:, 0].astype(F32))
    return estimate * summed / cover_count


def solution(mesh):
    placed = (
        P("stack", "brick", None),
        P(None, "stack", "brick", None),
        P(),
        P(),
        P(None, "brick"),
    )
    return jax.shard_map(
        shards, mesh=mesh, in_specs=placed, out_specs=P("stack", "brick", None), check_vma=False
    )
```

```python
import functools

import jax
import jax.numpy as jnp
from jax import lax
from jax.experimental import pallas as pl
from jax.experimental.pallas import tpu as pltpu
from jax.sharding import PartitionSpec as P

F32, BF16 = jnp.float32, jnp.bfloat16
ROW = 8
DIRECT = 2


def split(values):
    high = values.astype(BF16)
    return high, (values - high.astype(F32)).astype(BF16)


def dot(left, right):
    return jnp.dot(left, right, preferred_element_type=F32)


def normal(taps_ref, view, dim):
    count = taps_ref.shape[2]
    total = taps_ref[view, dim, 0]
    for t in range(1, count):
        total = total + taps_ref[view, dim, t]
    scale = 1.0 / jnp.full((8, 128), total, F32)
    return [jnp.full((8, 128), taps_ref[view, dim, t], F32) * scale for t in range(count)]


def prepare_kernel(half, rows, wide, taps_ref, lateral_ref, lateral_back_ref, across_ref, across_back_ref):
    views, width = taps_ref.shape[0], 128

    def banded(taps, lane_of, count):
        lane = lax.broadcasted_iota(jnp.int32, (8, width), 1)
        first = jnp.zeros((8, width), F32)
        for t, tap in enumerate(taps):
            first = jnp.where(lane == lane_of(t) % width, tap, first)
        tall = jnp.concatenate([first] * (count // 8), axis=0)
        return pltpu.roll(tall, 0, 1, stride=1, stride_axis=0)

    row = lax.broadcasted_iota(jnp.int32, (width, width), 0)
    lane = lax.broadcasted_iota(jnp.int32, (width, width), 1)
    near = jnp.abs(row - lane) <= half
    back = [[jnp.zeros((wide, width), F32)] for _ in range(-(-views * rows // width))]
    for view in range(views):
        taps = normal(taps_ref, view, 2)
        for ref, lane_of in ((across_ref, lambda t: half - t), (across_back_ref, lambda t: t - half)):
            high, low = split(jnp.where(near, banded(taps, lane_of, width), 0.0))
            ref[view, :width, :width] = high
            ref[view, :width, width:] = low
            ref[view, width:, :width] = high
            ref[view, width:, width:] = jnp.zeros_like(low)
        taps = normal(taps_ref, view, 1)
        high, low = split(banded(taps, lambda t: t + 1, rows))
        high = high.astype(F32)
        at = slice(view * rows, (view + 1) * rows)
        lateral_ref[at, : 2 * wide] = (high + pltpu.roll(high, wide, 1)).astype(BF16)
        lateral_ref[at, 2 * wide :] = low[:, :wide]
        field = jnp.where(lane[:wide] < rows, banded(taps, lambda t: -1 - t, wide), 0.0)
        place = view * rows
        shift = place % width
        back[place // width].append(pltpu.roll(field, shift, 1) if shift else field)
    for block, fields in enumerate(back):
        total = fields[0]
        for field in fields[1:]:
            total = total + field
        high, low = split(total)
        size = min(width, views * rows - block * width)
        lateral_back_ref[:wide, block * width : block * width + size] = high[:, :size]
        lateral_back_ref[wide:, block * width : block * width + size] = low[:, :size]


def pair_of(ref, z):
    first_h, first_l = split(ref[z])
    second_h, second_l = split(ref[z + 1])
    return jnp.concatenate([first_h, second_h], axis=1), jnp.concatenate([first_l, second_l], axis=1)


def across_pass(field, matrix):
    depth, rows, width = field.shape
    upper, lower = split(field.reshape(depth * rows, width))
    both = dot(jnp.concatenate([upper, lower], axis=1), matrix)
    return (both[:, :width] + both[:, width:]).reshape(depth, rows, width)


def forward_kernel(half, taps_ref, low_ref, mid_ref, high_ref, lateral_ref, across_ref, out_ref, wide_ref):
    views, depth, rows, width = out_ref.shape
    for part, ref in enumerate((low_ref, mid_ref, high_ref)):

        def lateral(pair, carry, part=part, ref=ref):
            upper, lower = pair_of(ref, pair * 2)
            result = dot(lateral_ref[...], jnp.concatenate([upper, lower, upper], axis=0))
            wide_ref[part * depth + pair * 2] = result[:, :width]
            wide_ref[part * depth + pair * 2 + 1] = result[:, width:]
            return carry

        lax.fori_loop(0, depth // 2, lateral, 0, unroll=True)

    start, block = depth - half, 8

    def axial(view, carry):
        taps = normal(taps_ref, view, 0)
        for group in range(rows // 8):
            at = pl.ds(pl.multiple_of(view * rows + group * 8, 8), 8)
            for base in range(0, depth, block):
                totals = [None] * block
                for z in range(base, base + block + len(taps) - 1):
                    field = wide_ref[start + z, at, :]
                    for i in range(block):
                        t = z - base - i
                        if 0 <= t < len(taps):
                            term = taps[t] * field
                            totals[i] = term if totals[i] is None else totals[i] + term
                for i in range(block):
                    out_ref[view, base + i, group * 8 : group * 8 + 8, :] = totals[i]
        return carry

    lax.fori_loop(0, views, axial, 0)
    for view in range(views):
        out_ref[view] = across_pass(out_ref[view], across_ref[view])


def axial_back(half, taps_ref, near_ref, wide_ref, places):
    views, depth, rows, width = near_ref.shape
    start = depth - half

    def body(view, carry):
        taps = normal(taps_ref, view, 0)
        for group in range(rows // 8):
            into = pl.ds(pl.multiple_of(view * rows + group * 8, 8), 8)
            field = [near_ref[view, z, group * 8 : group * 8 + 8, :] for z in range(depth)]
            for slot, z in enumerate(places):
                total = None
                for source in range(depth):
                    t = z - start - source
                    if 0 <= t < len(taps):
                        term = taps[t] * field[source]
                        total = term if total is None else total + term
                wide_ref[slot, into, :] = jnp.zeros((8, width), F32) if total is None else total
        return carry

    lax.fori_loop(0, views, body, 0)


def lateral_back(lateral_ref, wide_ref, first, out_ref):
    depth, wide, width = out_ref.shape

    def body(pair, carry):
        upper, lower = pair_of(wide_ref, first + pair * 2)
        one = dot(lateral_ref[...], upper)
        result = one[:wide] + one[wide:] + dot(lateral_ref[:wide], lower)
        out_ref[pair * 2] = result[:, :width]
        out_ref[pair * 2 + 1] = result[:, width:]
        return carry

    lax.fori_loop(0, depth // 2, body, 0, unroll=True)


def outer_kernel(half, taps_ref, cover_ref, order_ref, *refs):
    tiles_ref, *direct = refs[:-7]
    blurred_ref, across_ref, lateral_ref, near_ref, low_ref, high_ref, wide_ref = refs[-7:]
    views, depth, rows, width = blurred_ref.shape
    halves, spread = tiles_ref.shape[1:3]
    for slot in range(views):
        view = order_ref[slot]
        if slot < spread:
            owned = jnp.concatenate([tiles_ref[:, part, slot] for part in range(halves)], axis=1)
        else:
            owned = direct[slot - spread][...]
        ratio = cover_ref[view].astype(F32) * owned / blurred_ref[view]
        near_ref[view] = across_pass(ratio, across_ref[view])
    axial_back(half, taps_ref, near_ref, wide_ref, list(range(depth)) + list(range(2 * depth, 3 * depth)))
    lateral_back(lateral_ref, wide_ref, 0, low_ref)
    lateral_back(lateral_ref, wide_ref, depth, high_ref)


def inner_kernel(half, taps_ref, near_ref, lateral_ref, mid_ref, wide_ref):
    depth = near_ref.shape[1]
    axial_back(half, taps_ref, near_ref, wide_ref, list(range(depth, 2 * depth)))
    lateral_back(lateral_ref, wide_ref, 0, mid_ref)


def turn_kernel(ring, offsets_ref, in_ref, out_ref):
    views = in_ref.shape[1]

    def body(place, carry):
        for view in range(views):
            source = lax.rem(place + ring - offsets_ref[view], ring)
            out_ref[place, view] = in_ref[source, view]
        return carry

    lax.fori_loop(0, ring, body, 0)


def pick_kernel(row, columns, offsets_ref, in_ref, order_ref, sorted_ref, pieces_ref, *direct):
    views = in_ref.shape[0]
    spread = pieces_ref.shape[1]
    cost, moves = [], []
    for view in range(views):
        move = lax.rem(offsets_ref[view], row * columns)
        across, along = lax.rem(move, row), move // row
        near = 2 * jnp.minimum(along, columns - along)
        far = 2 * jnp.minimum(along + 1, columns - 1 - along)
        far = jnp.where(across > 0, far, 0)
        cost.append(jnp.maximum(jnp.minimum(across, row - across), jnp.maximum(near, far)))
        moves.append(move)
    for view in range(views):
        rank = jnp.int32(0)
        for other in range(views):
            if other != view:
                ahead = cost[other] >= cost[view] if other < view else cost[other] > cost[view]
                rank = rank + ahead.astype(jnp.int32)
        order_ref[rank] = jnp.int32(view)
        sorted_ref[rank] = moves[view]
    for slot in range(views):
        view = order_ref[slot]
        if slot < spread:
            pieces_ref[:, slot] = in_ref[view]
        else:
            direct[slot - spread][...] = in_ref[view].reshape(direct[slot - spread].shape)


SMEM = pl.BlockSpec(memory_space=pltpu.SMEM)
VMEM = pl.BlockSpec(memory_space=pltpu.VMEM)
PARAMS = pltpu.CompilerParams(vmem_limit_bytes=48 << 20)


def call(kernel, name, outs, scalars, arrays, scratch=(), out_specs=None):
    return pl.pallas_call(
        kernel,
        out_shape=tuple(jax.ShapeDtypeStruct(shape, dtype) for shape, dtype in outs),
        in_specs=[SMEM] * len(scalars) + [VMEM] * len(arrays),
        out_specs=tuple(out_specs or [VMEM] * len(outs)),
        scratch_shapes=[pltpu.VMEM(shape, F32) for shape in scratch],
        compiler_params=PARAMS,
        name=name,
    )(*scalars, *arrays)


def shards(estimate, view_data, psf_taps, offsets, coverage):
    depth, rows, width = estimate.shape
    views = view_data.shape[0]
    half = (psf_taps.shape[2] - 1) // 2
    reach = half + 1
    wide = rows + 2 * reach
    ring = lax.axis_size("brick")
    stacks = lax.axis_size("stack")
    up = [(i, i + 1) for i in range(stacks - 1)]
    down = [(i + 1, i) for i in range(stacks - 1)]
    right = [(i, i + 1) for i in range(ring - 1)]
    left = [(i + 1, i) for i in range(ring - 1)]

    parts = ring // depth
    strip = rows // parts
    spread_views = views - DIRECT
    order, moves, pieces, *straight = call(
        functools.partial(pick_kernel, ROW, ring // ROW),
        "pick",
        [((views,), jnp.int32)] * 2 + [((ring, spread_views, strip, width), F32)] + [((depth, rows, width), F32)] * DIRECT,
        [offsets],
        [view_data.reshape(views, ring, strip, width)],
        out_specs=[SMEM, SMEM] + [VMEM] * (1 + DIRECT),
    )
    spread = lax.all_to_all(pieces, "brick", 0, 0, tiled=True)

    head = lax.ppermute(estimate[:, rows - reach :], "brick", right)
    tail = lax.ppermute(estimate[:, :reach], "brick", left)
    mid = jnp.concatenate([head, estimate, tail], axis=1)
    low = lax.ppermute(mid, "stack", up)
    high = lax.ppermute(mid, "stack", down)

    lateral_on, lateral_off, across_on, across_off = call(
        functools.partial(prepare_kernel, half, rows, wide),
        "prepare",
        [((views * rows, 3 * wide), BF16), ((2 * wide, views * rows), BF16)] + [((views, 2 * width, 2 * width), BF16)] * 2,
        [psf_taps],
        [],
    )

    hops = [lambda x: x]
    for by in range(1, ring):
        pairs = [(i, (i + by) % ring) for i in range(ring)]
        hops.append(functools.partial(lax.ppermute, axis_name="brick", perm=pairs))

    def send(slot, x):
        return lax.switch(moves[spread_views + slot], hops, x)

    first = send(0, straight[0])
    spread, first = lax.optimization_barrier((spread, first))
    (turned,) = call(functools.partial(turn_kernel, ring), "turn", [(spread.shape, F32)], [moves], [spread])
    turned, low, mid, high, *waiting = lax.optimization_barrier((turned, low, mid, high, *straight[1:]))
    tiles = lax.all_to_all(turned, "brick", 0, 0, tiled=True)
    tiles = tiles.reshape(depth, parts, spread_views, strip, width)
    sent = [first] + [send(slot + 1, x) for slot, x in enumerate(waiting)]

    (blurred,) = call(
        functools.partial(forward_kernel, half),
        "forward",
        [((views, depth, rows, width), F32)],
        [psf_taps],
        [low, mid, high, lateral_on, across_on],
        [(3 * depth, views * rows, width)],
    )

    slab = ((depth, wide, width), F32)
    near, below, above = call(
        functools.partial(outer_kernel, half),
        "outer",
        [((views, depth, rows, width), F32), slab, slab],
        [psf_taps, coverage[:, 0], order],
        [tiles, *sent, blurred, across_off, lateral_off],
        [(2 * depth, views * rows, width)],
    )
    from_above = lax.ppermute(below, "stack", down)
    from_below = lax.ppermute(above, "stack", up)
    (own,) = call(
        functools.partial(inner_kernel, half),
        "inner",
        [slab],
        [psf_taps],
        [near, lateral_off],
        [(depth, views * rows, width)],
    )

    total = own + from_above + from_below
    from_right = lax.ppermute(total[:, :reach], "brick", left)
    from_left = lax.ppermute(total[:, rows + reach :], "brick", right)
    summed = total[:, reach : rows + reach]
    gap = jnp.zeros((depth, rows - reach, width), F32)
    summed = summed + jnp.concatenate([from_left, gap], axis=1) + jnp.concatenate([gap, from_right], axis=1)
    cover_count = jnp.sum(coverage[:, 0].astype(F32))
    return estimate * summed / cover_count


def solution(mesh):
    placed = (
        P("stack", "brick", None),
        P(None, "stack", "brick", None),
        P(),
        P(),
        P(None, "brick"),
    )
    return jax.shard_map(
        shards, mesh=mesh, in_specs=placed, out_specs=P("stack", "brick", None), check_vma=False
    )
```

```python
import functools

import jax
import jax.numpy as jnp
from jax import lax
from jax.experimental import pallas as pl
from jax.experimental.pallas import tpu as pltpu
from jax.sharding import PartitionSpec as P

F32, BF16 = jnp.float32, jnp.bfloat16


def split(values):
    high = values.astype(BF16)
    return high, (values - high.astype(F32)).astype(BF16)


def dot(left, right):
    return jnp.dot(left, right, preferred_element_type=F32)


def normal(taps_ref, view, dim):
    count = taps_ref.shape[2]
    total = taps_ref[view, dim, 0]
    for t in range(1, count):
        total = total + taps_ref[view, dim, t]
    scale = 1.0 / jnp.full((8, 128), total, F32)
    return [jnp.full((8, 128), taps_ref[view, dim, t], F32) * scale for t in range(count)]


def prepare_kernel(half, rows, wide, taps_ref, lateral_ref, lateral_back_ref, across_ref, across_back_ref):
    views, width = taps_ref.shape[0], 128

    def banded(taps, lane_of, count):
        lane = lax.broadcasted_iota(jnp.int32, (8, width), 1)
        first = jnp.zeros((8, width), F32)
        for t, tap in enumerate(taps):
            first = jnp.where(lane == lane_of(t) % width, tap, first)
        tall = jnp.concatenate([first] * (count // 8), axis=0)
        return pltpu.roll(tall, 0, 1, stride=1, stride_axis=0)

    row = lax.broadcasted_iota(jnp.int32, (width, width), 0)
    lane = lax.broadcasted_iota(jnp.int32, (width, width), 1)
    near = jnp.abs(row - lane) <= half
    back = [[jnp.zeros((wide, width), F32)] for _ in range(-(-views * rows // width))]
    for view in range(views):
        taps = normal(taps_ref, view, 2)
        for ref, lane_of in ((across_ref, lambda t: half - t), (across_back_ref, lambda t: t - half)):
            high, low = split(jnp.where(near, banded(taps, lane_of, width), 0.0))
            ref[view, :width, :width] = high
            ref[view, :width, width:] = low
            ref[view, width:, :width] = high
            ref[view, width:, width:] = jnp.zeros_like(low)
        taps = normal(taps_ref, view, 1)
        high, low = split(banded(taps, lambda t: t + 1, rows))
        high = high.astype(F32)
        at = slice(view * rows, (view + 1) * rows)
        lateral_ref[at, : 2 * wide] = (high + pltpu.roll(high, wide, 1)).astype(BF16)
        lateral_ref[at, 2 * wide :] = low[:, :wide]
        field = jnp.where(lane[:wide] < rows, banded(taps, lambda t: -1 - t, wide), 0.0)
        place = view * rows
        shift = place % width
        back[place // width].append(pltpu.roll(field, shift, 1) if shift else field)
    for block, fields in enumerate(back):
        total = fields[0]
        for field in fields[1:]:
            total = total + field
        high, low = split(total)
        size = min(width, views * rows - block * width)
        lateral_back_ref[:wide, block * width : block * width + size] = high[:, :size]
        lateral_back_ref[wide:, block * width : block * width + size] = low[:, :size]


def pair_of(ref, z):
    first_h, first_l = split(ref[z])
    second_h, second_l = split(ref[z + 1])
    return jnp.concatenate([first_h, second_h], axis=1), jnp.concatenate([first_l, second_l], axis=1)


def across_pass(field, matrix):
    depth, rows, width = field.shape
    upper, lower = split(field.reshape(depth * rows, width))
    both = dot(jnp.concatenate([upper, lower], axis=1), matrix)
    return (both[:, :width] + both[:, width:]).reshape(depth, rows, width)


def forward_kernel(half, taps_ref, low_ref, mid_ref, high_ref, lateral_ref, across_ref, out_ref, wide_ref):
    views, depth, rows, width = out_ref.shape
    for part, ref in enumerate((low_ref, mid_ref, high_ref)):

        def lateral(pair, carry, part=part, ref=ref):
            upper, lower = pair_of(ref, pair * 2)
            result = dot(lateral_ref[...], jnp.concatenate([upper, lower, upper], axis=0))
            wide_ref[part * depth + pair * 2] = result[:, :width]
            wide_ref[part * depth + pair * 2 + 1] = result[:, width:]
            return carry

        lax.fori_loop(0, depth // 2, lateral, 0, unroll=True)

    start, block = depth - half, 8

    def axial(view, carry):
        taps = normal(taps_ref, view, 0)
        for group in range(rows // 8):
            at = pl.ds(pl.multiple_of(view * rows + group * 8, 8), 8)
            for base in range(0, depth, block):
                totals = [None] * block
                for z in range(base, base + block + len(taps) - 1):
                    field = wide_ref[start + z, at, :]
                    for i in range(block):
                        t = z - base - i
                        if 0 <= t < len(taps):
                            term = taps[t] * field
                            totals[i] = term if totals[i] is None else totals[i] + term
                for i in range(block):
                    out_ref[view, base + i, group * 8 : group * 8 + 8, :] = totals[i]
        return carry

    lax.fori_loop(0, views, axial, 0)
    for view in range(views):
        out_ref[view] = across_pass(out_ref[view], across_ref[view])


def axial_back(half, taps_ref, near_ref, wide_ref, places):
    views, depth, rows, width = near_ref.shape
    start = depth - half

    def body(view, carry):
        taps = normal(taps_ref, view, 0)
        for group in range(rows // 8):
            into = pl.ds(pl.multiple_of(view * rows + group * 8, 8), 8)
            field = [near_ref[view, z, group * 8 : group * 8 + 8, :] for z in range(depth)]
            for slot, z in enumerate(places):
                total = None
                for source in range(depth):
                    t = z - start - source
                    if 0 <= t < len(taps):
                        term = taps[t] * field[source]
                        total = term if total is None else total + term
                wide_ref[slot, into, :] = jnp.zeros((8, width), F32) if total is None else total
        return carry

    lax.fori_loop(0, views, body, 0)


def lateral_back(lateral_ref, wide_ref, first, out_ref):
    depth, wide, width = out_ref.shape

    def body(pair, carry):
        upper, lower = pair_of(wide_ref, first + pair * 2)
        one = dot(lateral_ref[...], upper)
        result = one[:wide] + one[wide:] + dot(lateral_ref[:wide], lower)
        out_ref[pair * 2] = result[:, :width]
        out_ref[pair * 2 + 1] = result[:, width:]
        return carry

    lax.fori_loop(0, depth // 2, body, 0, unroll=True)


def outer_kernel(half, taps_ref, cover_ref, tiles_ref, blurred_ref, across_ref, lateral_ref, near_ref, low_ref, high_ref, wide_ref):
    views, depth, rows, width = blurred_ref.shape
    for view in range(views):
        owned = jnp.concatenate([tiles_ref[:, part, view] for part in range(tiles_ref.shape[1])], axis=1)
        ratio = cover_ref[view].astype(F32) * owned / blurred_ref[view]
        near_ref[view] = across_pass(ratio, across_ref[view])
    axial_back(half, taps_ref, near_ref, wide_ref, list(range(depth)) + list(range(2 * depth, 3 * depth)))
    lateral_back(lateral_ref, wide_ref, 0, low_ref)
    lateral_back(lateral_ref, wide_ref, depth, high_ref)


def inner_kernel(half, taps_ref, near_ref, lateral_ref, mid_ref, wide_ref):
    depth = near_ref.shape[1]
    axial_back(half, taps_ref, near_ref, wide_ref, list(range(depth, 2 * depth)))
    lateral_back(lateral_ref, wide_ref, 0, mid_ref)


def turn_kernel(ring, offsets_ref, in_ref, out_ref):
    views = in_ref.shape[1]

    def body(place, carry):
        for view in range(views):
            source = lax.rem(place + ring - lax.rem(offsets_ref[view], ring), ring)
            out_ref[place, view] = in_ref[source, view]
        return carry

    lax.fori_loop(0, ring, body, 0)


def pieces_kernel(in_ref, out_ref, sems):
    copies = [pltpu.make_async_copy(in_ref.at[view], out_ref.at[:, view], sems.at[view]) for view in range(in_ref.shape[0])]
    for copy in copies:
        copy.start()
    for copy in copies:
        copy.wait()


SMEM = pl.BlockSpec(memory_space=pltpu.SMEM)
VMEM = pl.BlockSpec(memory_space=pltpu.VMEM)
PARAMS = pltpu.CompilerParams(vmem_limit_bytes=48 << 20)


def call(kernel, name, outs, scalars, arrays, scratch=(), out_specs=None):
    return pl.pallas_call(
        kernel,
        out_shape=tuple(jax.ShapeDtypeStruct(shape, dtype) for shape, dtype in outs),
        in_specs=[SMEM] * len(scalars) + [VMEM] * len(arrays),
        out_specs=tuple(out_specs or [VMEM] * len(outs)),
        scratch_shapes=[pltpu.VMEM(shape, F32) for shape in scratch],
        compiler_params=PARAMS,
        name=name,
    )(*scalars, *arrays)


def shards(estimate, view_data, psf_taps, offsets, coverage):
    depth, rows, width = estimate.shape
    views = view_data.shape[0]
    half = (psf_taps.shape[2] - 1) // 2
    reach = half + 1
    wide = rows + 2 * reach
    ring = lax.axis_size("brick")
    stacks = lax.axis_size("stack")
    up = [(i, i + 1) for i in range(stacks - 1)]
    down = [(i + 1, i) for i in range(stacks - 1)]
    right = [(i, i + 1) for i in range(ring - 1)]
    left = [(i + 1, i) for i in range(ring - 1)]

    parts = ring // depth
    strip = rows // parts
    pieces = pl.pallas_call(
        pieces_kernel,
        out_shape=jax.ShapeDtypeStruct((ring, views, strip, width), F32),
        in_specs=[pl.BlockSpec(memory_space=pltpu.HBM)],
        out_specs=VMEM,
        scratch_shapes=[pltpu.SemaphoreType.DMA((views,))],
        compiler_params=PARAMS,
        name="pieces",
    )(view_data.reshape(views, ring, strip, width))

    head = lax.ppermute(estimate[:, rows - reach :], "brick", right)
    tail = lax.ppermute(estimate[:, :reach], "brick", left)
    pieces, head, tail = lax.optimization_barrier((pieces, head, tail))
    spread = lax.all_to_all(pieces, "brick", 0, 0, tiled=True)
    mid = jnp.concatenate([head, estimate, tail], axis=1)
    low = lax.ppermute(mid, "stack", up)
    high = lax.ppermute(mid, "stack", down)

    lateral_on, lateral_off, across_on, across_off = call(
        functools.partial(prepare_kernel, half, rows, wide),
        "prepare",
        [((views * rows, 3 * wide), BF16), ((2 * wide, views * rows), BF16)] + [((views, 2 * width, 2 * width), BF16)] * 2,
        [psf_taps],
        [],
    )

    spread, low, high = lax.optimization_barrier((spread, low, high))
    (turned,) = call(functools.partial(turn_kernel, ring), "turn", [(spread.shape, F32)], [offsets], [spread])
    tiles = lax.all_to_all(turned, "brick", 0, 0, tiled=True)
    tiles = tiles.reshape(depth, parts, views, strip, width)

    (blurred,) = call(
        functools.partial(forward_kernel, half),
        "forward",
        [((views, depth, rows, width), F32)],
        [psf_taps],
        [low, mid, high, lateral_on, across_on],
        [(3 * depth, views * rows, width)],
    )

    slab = ((depth, wide, width), F32)
    near, below, above = call(
        functools.partial(outer_kernel, half),
        "outer",
        [((views, depth, rows, width), F32), slab, slab],
        [psf_taps, coverage[:, 0]],
        [tiles, blurred, across_off, lateral_off],
        [(2 * depth, views * rows, width)],
    )
    from_above = lax.ppermute(below, "stack", down)
    from_below = lax.ppermute(above, "stack", up)
    (own,) = call(
        functools.partial(inner_kernel, half),
        "inner",
        [slab],
        [psf_taps],
        [near, lateral_off],
        [(depth, views * rows, width)],
    )

    total = own + from_above + from_below
    from_right = lax.ppermute(total[:, :reach], "brick", left)
    from_left = lax.ppermute(total[:, rows + reach :], "brick", right)
    summed = total[:, reach : rows + reach]
    gap = jnp.zeros((depth, rows - reach, width), F32)
    summed = summed + jnp.concatenate([from_left, gap], axis=1) + jnp.concatenate([gap, from_right], axis=1)
    cover_count = jnp.sum(coverage[:, 0].astype(F32))
    return estimate * summed / cover_count


def solution(mesh):
    placed = (
        P("stack", "brick", None),
        P(None, "stack", "brick", None),
        P(),
        P(),
        P(None, "brick"),
    )
    return jax.shard_map(
        shards, mesh=mesh, in_specs=placed, out_specs=P("stack", "brick", None), check_vma=False
    )
```

```python
import functools

import jax
import jax.numpy as jnp
from jax import lax
from jax.experimental import pallas as pl
from jax.experimental.pallas import tpu as pltpu
from jax.sharding import PartitionSpec as P

F32, BF16 = jnp.float32, jnp.bfloat16
ROW = 8
DIRECT = 2
EARLY = 1


def split(values):
    high = values.astype(BF16)
    return high, (values - high.astype(F32)).astype(BF16)


def dot(left, right):
    return jnp.dot(left, right, preferred_element_type=F32)


def normal(taps_ref, view, dim):
    count = taps_ref.shape[2]
    total = taps_ref[view, dim, 0]
    for t in range(1, count):
        total = total + taps_ref[view, dim, t]
    scale = 1.0 / jnp.full((8, 128), total, F32)
    return [jnp.full((8, 128), taps_ref[view, dim, t], F32) * scale for t in range(count)]


def prepare_kernel(half, rows, wide, taps_ref, lateral_ref, lateral_back_ref, across_ref, across_back_ref):
    views, width = taps_ref.shape[0], 128

    def banded(taps, lane_of, count):
        lane = lax.broadcasted_iota(jnp.int32, (8, width), 1)
        first = jnp.zeros((8, width), F32)
        for t, tap in enumerate(taps):
            first = jnp.where(lane == lane_of(t) % width, tap, first)
        tall = jnp.concatenate([first] * (count // 8), axis=0)
        return pltpu.roll(tall, 0, 1, stride=1, stride_axis=0)

    row = lax.broadcasted_iota(jnp.int32, (width, width), 0)
    lane = lax.broadcasted_iota(jnp.int32, (width, width), 1)
    near = jnp.abs(row - lane) <= half
    back = [[jnp.zeros((wide, width), F32)] for _ in range(-(-views * rows // width))]
    for view in range(views):
        taps = normal(taps_ref, view, 2)
        for ref, lane_of in ((across_ref, lambda t: half - t), (across_back_ref, lambda t: t - half)):
            high, low = split(jnp.where(near, banded(taps, lane_of, width), 0.0))
            ref[view, :width, :width] = high
            ref[view, :width, width:] = low
            ref[view, width:, :width] = high
            ref[view, width:, width:] = jnp.zeros_like(low)
        taps = normal(taps_ref, view, 1)
        high, low = split(banded(taps, lambda t: t + 1, rows))
        high = high.astype(F32)
        at = slice(view * rows, (view + 1) * rows)
        lateral_ref[at, : 2 * wide] = (high + pltpu.roll(high, wide, 1)).astype(BF16)
        lateral_ref[at, 2 * wide :] = low[:, :wide]
        field = jnp.where(lane[:wide] < rows, banded(taps, lambda t: -1 - t, wide), 0.0)
        place = view * rows
        shift = place % width
        back[place // width].append(pltpu.roll(field, shift, 1) if shift else field)
    for block, fields in enumerate(back):
        total = fields[0]
        for field in fields[1:]:
            total = total + field
        high, low = split(total)
        size = min(width, views * rows - block * width)
        lateral_back_ref[:wide, block * width : block * width + size] = high[:, :size]
        lateral_back_ref[wide:, block * width : block * width + size] = low[:, :size]


def pair_of(ref, z):
    first_h, first_l = split(ref[z])
    second_h, second_l = split(ref[z + 1])
    return jnp.concatenate([first_h, second_h], axis=1), jnp.concatenate([first_l, second_l], axis=1)


def across_pass(field, matrix):
    depth, rows, width = field.shape
    upper, lower = split(field.reshape(depth * rows, width))
    both = dot(jnp.concatenate([upper, lower], axis=1), matrix)
    return (both[:, :width] + both[:, width:]).reshape(depth, rows, width)


def forward_kernel(half, taps_ref, low_ref, mid_ref, high_ref, lateral_ref, across_ref, out_ref, wide_ref):
    views, depth, rows, width = out_ref.shape
    for part, ref in enumerate((low_ref, mid_ref, high_ref)):

        def lateral(pair, carry, part=part, ref=ref):
            upper, lower = pair_of(ref, pair * 2)
            result = dot(lateral_ref[...], jnp.concatenate([upper, lower, upper], axis=0))
            wide_ref[part * depth + pair * 2] = result[:, :width]
            wide_ref[part * depth + pair * 2 + 1] = result[:, width:]
            return carry

        lax.fori_loop(0, depth // 2, lateral, 0, unroll=True)

    start, block = depth - half, 8

    def axial(view, carry):
        taps = normal(taps_ref, view, 0)
        for group in range(rows // 8):
            at = pl.ds(pl.multiple_of(view * rows + group * 8, 8), 8)
            for base in range(0, depth, block):
                totals = [None] * block
                for z in range(base, base + block + len(taps) - 1):
                    field = wide_ref[start + z, at, :]
                    for i in range(block):
                        t = z - base - i
                        if 0 <= t < len(taps):
                            term = taps[t] * field
                            totals[i] = term if totals[i] is None else totals[i] + term
                for i in range(block):
                    out_ref[view, base + i, group * 8 : group * 8 + 8, :] = totals[i]
        return carry

    lax.fori_loop(0, views, axial, 0)
    for view in range(views):
        out_ref[view] = across_pass(out_ref[view], across_ref[view])


def axial_back(half, taps_ref, near_ref, wide_ref, places):
    views, depth, rows, width = near_ref.shape
    start = depth - half

    def body(view, carry):
        taps = normal(taps_ref, view, 0)
        for group in range(rows // 8):
            into = pl.ds(pl.multiple_of(view * rows + group * 8, 8), 8)
            field = [near_ref[view, z, group * 8 : group * 8 + 8, :] for z in range(depth)]
            for slot, z in enumerate(places):
                total = None
                for source in range(depth):
                    t = z - start - source
                    if 0 <= t < len(taps):
                        term = taps[t] * field[source]
                        total = term if total is None else total + term
                wide_ref[slot, into, :] = jnp.zeros((8, width), F32) if total is None else total
        return carry

    lax.fori_loop(0, views, body, 0)


def lateral_back(lateral_ref, wide_ref, first, out_ref):
    depth, wide, width = out_ref.shape

    def body(pair, carry):
        upper, lower = pair_of(wide_ref, first + pair * 2)
        one = dot(lateral_ref[...], upper)
        result = one[:wide] + one[wide:] + dot(lateral_ref[:wide], lower)
        out_ref[pair * 2] = result[:, :width]
        out_ref[pair * 2 + 1] = result[:, width:]
        return carry

    lax.fori_loop(0, depth // 2, body, 0, unroll=True)


def outer_kernel(half, taps_ref, cover_ref, order_ref, *refs):
    tiles_ref, *direct = refs[:-7]
    blurred_ref, across_ref, lateral_ref, near_ref, low_ref, high_ref, wide_ref = refs[-7:]
    views, depth, rows, width = blurred_ref.shape
    halves, spread = tiles_ref.shape[1:3]
    for slot in range(views):
        view = order_ref[slot]
        if slot < spread:
            owned = jnp.concatenate([tiles_ref[:, part, slot] for part in range(halves)], axis=1)
        else:
            owned = direct[slot - spread][...]
        ratio = cover_ref[view].astype(F32) * owned / blurred_ref[view]
        near_ref[view] = across_pass(ratio, across_ref[view])
    axial_back(half, taps_ref, near_ref, wide_ref, list(range(depth)) + list(range(2 * depth, 3 * depth)))
    lateral_back(lateral_ref, wide_ref, 0, low_ref)
    lateral_back(lateral_ref, wide_ref, depth, high_ref)


def inner_kernel(half, taps_ref, near_ref, lateral_ref, mid_ref, wide_ref):
    depth = near_ref.shape[1]
    axial_back(half, taps_ref, near_ref, wide_ref, list(range(depth, 2 * depth)))
    lateral_back(lateral_ref, wide_ref, 0, mid_ref)


def turn_kernel(ring, offsets_ref, in_ref, out_ref):
    views = in_ref.shape[1]

    def body(place, carry):
        for view in range(views):
            source = lax.rem(place + ring - offsets_ref[view], ring)
            out_ref[place, view] = in_ref[source, view]
        return carry

    lax.fori_loop(0, ring, body, 0)


def pick_kernel(row, columns, offsets_ref, in_ref, order_ref, sorted_ref, pieces_ref, *direct):
    views = in_ref.shape[0]
    spread = pieces_ref.shape[1]
    cost, moves = [], []
    for view in range(views):
        move = lax.rem(offsets_ref[view], row * columns)
        across, along = lax.rem(move, row), move // row
        near = 2 * jnp.minimum(along, columns - along)
        far = 2 * jnp.minimum(along + 1, columns - 1 - along)
        far = jnp.where(across > 0, far, 0)
        cost.append(jnp.maximum(jnp.minimum(across, row - across), jnp.maximum(near, far)))
        moves.append(move)
    for view in range(views):
        rank = jnp.int32(0)
        for other in range(views):
            if other != view:
                ahead = cost[other] >= cost[view] if other < view else cost[other] > cost[view]
                rank = rank + ahead.astype(jnp.int32)
        order_ref[rank] = jnp.int32(view)
        sorted_ref[rank] = moves[view]
    for slot in range(views):
        view = order_ref[slot]
        if slot < spread:
            pieces_ref[:, slot] = in_ref[view]
        else:
            direct[slot - spread][...] = in_ref[view].reshape(direct[slot - spread].shape)


SMEM = pl.BlockSpec(memory_space=pltpu.SMEM)
VMEM = pl.BlockSpec(memory_space=pltpu.VMEM)
PARAMS = pltpu.CompilerParams(vmem_limit_bytes=48 << 20)


def call(kernel, name, outs, scalars, arrays, scratch=(), out_specs=None):
    return pl.pallas_call(
        kernel,
        out_shape=tuple(jax.ShapeDtypeStruct(shape, dtype) for shape, dtype in outs),
        in_specs=[SMEM] * len(scalars) + [VMEM] * len(arrays),
        out_specs=tuple(out_specs or [VMEM] * len(outs)),
        scratch_shapes=[pltpu.VMEM(shape, F32) for shape in scratch],
        compiler_params=PARAMS,
        name=name,
    )(*scalars, *arrays)


def shards(estimate, view_data, psf_taps, offsets, coverage):
    depth, rows, width = estimate.shape
    views = view_data.shape[0]
    half = (psf_taps.shape[2] - 1) // 2
    reach = half + 1
    wide = rows + 2 * reach
    ring = lax.axis_size("brick")
    stacks = lax.axis_size("stack")
    up = [(i, i + 1) for i in range(stacks - 1)]
    down = [(i + 1, i) for i in range(stacks - 1)]
    right = [(i, i + 1) for i in range(ring - 1)]
    left = [(i + 1, i) for i in range(ring - 1)]

    parts = ring // depth
    strip = rows // parts
    spread_views = views - DIRECT
    order, moves, pieces, *straight = call(
        functools.partial(pick_kernel, ROW, ring // ROW),
        "pick",
        [((views,), jnp.int32)] * 2 + [((ring, spread_views, strip, width), F32)] + [((depth, rows, width), F32)] * DIRECT,
        [offsets],
        [view_data.reshape(views, ring, strip, width)],
        out_specs=[SMEM, SMEM] + [VMEM] * (1 + DIRECT),
    )
    head = lax.ppermute(estimate[:, rows - reach :], "brick", right)
    tail = lax.ppermute(estimate[:, :reach], "brick", left)
    pieces, head, tail = lax.optimization_barrier((pieces, head, tail))
    spread = lax.all_to_all(pieces, "brick", 0, 0, tiled=True)
    mid = jnp.concatenate([head, estimate, tail], axis=1)
    low = lax.ppermute(mid, "stack", up)
    high = lax.ppermute(mid, "stack", down)

    lateral_on, lateral_off, across_on, across_off = call(
        functools.partial(prepare_kernel, half, rows, wide),
        "prepare",
        [((views * rows, 3 * wide), BF16), ((2 * wide, views * rows), BF16)] + [((views, 2 * width, 2 * width), BF16)] * 2,
        [psf_taps],
        [],
    )

    hops = [lambda x: x]
    for by in range(1, ring):
        pairs = [(i, (i + by) % ring) for i in range(ring)]
        hops.append(functools.partial(lax.ppermute, axis_name="brick", perm=pairs))

    def send(slot, x):
        return lax.switch(moves[spread_views + slot], hops, x)

    sent = [send(slot, straight[slot]) for slot in range(EARLY)]
    spread, low, high, *sent = lax.optimization_barrier((spread, low, high, *sent))
    (turned,) = call(functools.partial(turn_kernel, ring), "turn", [(spread.shape, F32)], [moves], [spread])
    tiles = lax.all_to_all(turned, "brick", 0, 0, tiled=True)
    tiles = tiles.reshape(depth, parts, spread_views, strip, width)

    (blurred,) = call(
        functools.partial(forward_kernel, half),
        "forward",
        [((views, depth, rows, width), F32)],
        [psf_taps],
        [low, mid, high, lateral_on, across_on],
        [(3 * depth, views * rows, width)],
    )

    blurred, *waiting = lax.optimization_barrier((blurred, *straight[EARLY:]))
    sent += [send(EARLY + slot, x) for slot, x in enumerate(waiting)]

    slab = ((depth, wide, width), F32)
    near, below, above = call(
        functools.partial(outer_kernel, half),
        "outer",
        [((views, depth, rows, width), F32), slab, slab],
        [psf_taps, coverage[:, 0], order],
        [tiles, *sent, blurred, across_off, lateral_off],
        [(2 * depth, views * rows, width)],
    )
    from_above = lax.ppermute(below, "stack", down)
    from_below = lax.ppermute(above, "stack", up)
    (own,) = call(
        functools.partial(inner_kernel, half),
        "inner",
        [slab],
        [psf_taps],
        [near, lateral_off],
        [(depth, views * rows, width)],
    )

    total = own + from_above + from_below
    from_right = lax.ppermute(total[:, :reach], "brick", left)
    from_left = lax.ppermute(total[:, rows + reach :], "brick", right)
    summed = total[:, reach : rows + reach]
    gap = jnp.zeros((depth, rows - reach, width), F32)
    summed = summed + jnp.concatenate([from_left, gap], axis=1) + jnp.concatenate([gap, from_right], axis=1)
    cover_count = jnp.sum(coverage[:, 0].astype(F32))
    return estimate * summed / cover_count


def solution(mesh):
    placed = (
        P("stack", "brick", None),
        P(None, "stack", "brick", None),
        P(),
        P(),
        P(None, "brick"),
    )
    return jax.shard_map(
        shards, mesh=mesh, in_specs=placed, out_specs=P("stack", "brick", None), check_vma=False
    )
```

```python
import functools

import jax
import jax.numpy as jnp
from jax import lax
from jax.experimental import pallas as pl
from jax.experimental.pallas import tpu as pltpu
from jax.sharding import PartitionSpec as P

F32, BF16 = jnp.float32, jnp.bfloat16
ROW = 8
DIRECT = 2
EARLY = 2


def split(values):
    high = values.astype(BF16)
    return high, (values - high.astype(F32)).astype(BF16)


def dot(left, right):
    return jnp.dot(left, right, preferred_element_type=F32)


def normal(taps_ref, view, dim):
    count = taps_ref.shape[2]
    total = taps_ref[view, dim, 0]
    for t in range(1, count):
        total = total + taps_ref[view, dim, t]
    scale = 1.0 / jnp.full((8, 128), total, F32)
    return [jnp.full((8, 128), taps_ref[view, dim, t], F32) * scale for t in range(count)]


def prepare_kernel(half, rows, wide, taps_ref, lateral_ref, lateral_back_ref, across_ref, across_back_ref):
    views, width = taps_ref.shape[0], 128

    def banded(taps, lane_of, count):
        lane = lax.broadcasted_iota(jnp.int32, (8, width), 1)
        first = jnp.zeros((8, width), F32)
        for t, tap in enumerate(taps):
            first = jnp.where(lane == lane_of(t) % width, tap, first)
        tall = jnp.concatenate([first] * (count // 8), axis=0)
        return pltpu.roll(tall, 0, 1, stride=1, stride_axis=0)

    row = lax.broadcasted_iota(jnp.int32, (width, width), 0)
    lane = lax.broadcasted_iota(jnp.int32, (width, width), 1)
    near = jnp.abs(row - lane) <= half
    back = [[jnp.zeros((wide, width), F32)] for _ in range(-(-views * rows // width))]
    for view in range(views):
        taps = normal(taps_ref, view, 2)
        for ref, lane_of in ((across_ref, lambda t: half - t), (across_back_ref, lambda t: t - half)):
            high, low = split(jnp.where(near, banded(taps, lane_of, width), 0.0))
            ref[view, :width, :width] = high
            ref[view, :width, width:] = low
            ref[view, width:, :width] = high
            ref[view, width:, width:] = jnp.zeros_like(low)
        taps = normal(taps_ref, view, 1)
        high, low = split(banded(taps, lambda t: t + 1, rows))
        high = high.astype(F32)
        at = slice(view * rows, (view + 1) * rows)
        lateral_ref[at, : 2 * wide] = (high + pltpu.roll(high, wide, 1)).astype(BF16)
        lateral_ref[at, 2 * wide :] = low[:, :wide]
        field = jnp.where(lane[:wide] < rows, banded(taps, lambda t: -1 - t, wide), 0.0)
        place = view * rows
        shift = place % width
        back[place // width].append(pltpu.roll(field, shift, 1) if shift else field)
    for block, fields in enumerate(back):
        total = fields[0]
        for field in fields[1:]:
            total = total + field
        high, low = split(total)
        size = min(width, views * rows - block * width)
        lateral_back_ref[:wide, block * width : block * width + size] = high[:, :size]
        lateral_back_ref[wide:, block * width : block * width + size] = low[:, :size]


def pair_of(ref, z):
    first_h, first_l = split(ref[z])
    second_h, second_l = split(ref[z + 1])
    return jnp.concatenate([first_h, second_h], axis=1), jnp.concatenate([first_l, second_l], axis=1)


def across_pass(field, matrix):
    depth, rows, width = field.shape
    upper, lower = split(field.reshape(depth * rows, width))
    both = dot(jnp.concatenate([upper, lower], axis=1), matrix)
    return (both[:, :width] + both[:, width:]).reshape(depth, rows, width)


def forward_kernel(half, taps_ref, low_ref, mid_ref, high_ref, lateral_ref, across_ref, out_ref, wide_ref):
    views, depth, rows, width = out_ref.shape
    for part, ref in enumerate((low_ref, mid_ref, high_ref)):

        def lateral(pair, carry, part=part, ref=ref):
            upper, lower = pair_of(ref, pair * 2)
            result = dot(lateral_ref[...], jnp.concatenate([upper, lower, upper], axis=0))
            wide_ref[part * depth + pair * 2] = result[:, :width]
            wide_ref[part * depth + pair * 2 + 1] = result[:, width:]
            return carry

        lax.fori_loop(0, depth // 2, lateral, 0, unroll=True)

    start, block = depth - half, 8

    def axial(view, carry):
        taps = normal(taps_ref, view, 0)
        for group in range(rows // 8):
            at = pl.ds(pl.multiple_of(view * rows + group * 8, 8), 8)
            for base in range(0, depth, block):
                totals = [None] * block
                for z in range(base, base + block + len(taps) - 1):
                    field = wide_ref[start + z, at, :]
                    for i in range(block):
                        t = z - base - i
                        if 0 <= t < len(taps):
                            term = taps[t] * field
                            totals[i] = term if totals[i] is None else totals[i] + term
                for i in range(block):
                    out_ref[view, base + i, group * 8 : group * 8 + 8, :] = totals[i]
        return carry

    lax.fori_loop(0, views, axial, 0)
    for view in range(views):
        out_ref[view] = across_pass(out_ref[view], across_ref[view])


def axial_back(half, taps_ref, near_ref, wide_ref, places):
    views, depth, rows, width = near_ref.shape
    start = depth - half

    def body(view, carry):
        taps = normal(taps_ref, view, 0)
        for group in range(rows // 8):
            into = pl.ds(pl.multiple_of(view * rows + group * 8, 8), 8)
            field = [near_ref[view, z, group * 8 : group * 8 + 8, :] for z in range(depth)]
            for slot, z in enumerate(places):
                total = None
                for source in range(depth):
                    t = z - start - source
                    if 0 <= t < len(taps):
                        term = taps[t] * field[source]
                        total = term if total is None else total + term
                wide_ref[slot, into, :] = jnp.zeros((8, width), F32) if total is None else total
        return carry

    lax.fori_loop(0, views, body, 0)


def lateral_back(lateral_ref, wide_ref, first, out_ref):
    depth, wide, width = out_ref.shape

    def body(pair, carry):
        upper, lower = pair_of(wide_ref, first + pair * 2)
        one = dot(lateral_ref[...], upper)
        result = one[:wide] + one[wide:] + dot(lateral_ref[:wide], lower)
        out_ref[pair * 2] = result[:, :width]
        out_ref[pair * 2 + 1] = result[:, width:]
        return carry

    lax.fori_loop(0, depth // 2, body, 0, unroll=True)


def outer_kernel(half, taps_ref, cover_ref, order_ref, *refs):
    tiles_ref, *direct = refs[:-7]
    blurred_ref, across_ref, lateral_ref, near_ref, low_ref, high_ref, wide_ref = refs[-7:]
    views, depth, rows, width = blurred_ref.shape
    halves, spread = tiles_ref.shape[1:3]
    for slot in range(views):
        view = order_ref[slot]
        if slot < spread:
            owned = jnp.concatenate([tiles_ref[:, part, slot] for part in range(halves)], axis=1)
        else:
            owned = direct[slot - spread][...]
        ratio = cover_ref[view].astype(F32) * owned / blurred_ref[view]
        near_ref[view] = across_pass(ratio, across_ref[view])
    axial_back(half, taps_ref, near_ref, wide_ref, list(range(depth)) + list(range(2 * depth, 3 * depth)))
    lateral_back(lateral_ref, wide_ref, 0, low_ref)
    lateral_back(lateral_ref, wide_ref, depth, high_ref)


def inner_kernel(half, taps_ref, near_ref, lateral_ref, mid_ref, wide_ref):
    depth = near_ref.shape[1]
    axial_back(half, taps_ref, near_ref, wide_ref, list(range(depth, 2 * depth)))
    lateral_back(lateral_ref, wide_ref, 0, mid_ref)


def turn_kernel(ring, offsets_ref, in_ref, out_ref):
    views = in_ref.shape[1]

    def body(place, carry):
        for view in range(views):
            source = lax.rem(place + ring - offsets_ref[view], ring)
            out_ref[place, view] = in_ref[source, view]
        return carry

    lax.fori_loop(0, ring, body, 0)


def pick_kernel(row, columns, offsets_ref, in_ref, order_ref, sorted_ref, pieces_ref, *direct):
    views = in_ref.shape[0]
    spread = pieces_ref.shape[1]
    cost, moves = [], []
    for view in range(views):
        move = lax.rem(offsets_ref[view], row * columns)
        across, along = lax.rem(move, row), move // row
        near = 2 * jnp.minimum(along, columns - along)
        far = 2 * jnp.minimum(along + 1, columns - 1 - along)
        far = jnp.where(across > 0, far, 0)
        cost.append(jnp.maximum(jnp.minimum(across, row - across), jnp.maximum(near, far)))
        moves.append(move)
    for view in range(views):
        rank = jnp.int32(0)
        for other in range(views):
            if other != view:
                ahead = cost[other] >= cost[view] if other < view else cost[other] > cost[view]
                rank = rank + ahead.astype(jnp.int32)
        order_ref[rank] = jnp.int32(view)
        sorted_ref[rank] = moves[view]
    for slot in range(views):
        view = order_ref[slot]
        if slot < spread:
            pieces_ref[:, slot] = in_ref[view]
        else:
            direct[slot - spread][...] = in_ref[view].reshape(direct[slot - spread].shape)


SMEM = pl.BlockSpec(memory_space=pltpu.SMEM)
VMEM = pl.BlockSpec(memory_space=pltpu.VMEM)
PARAMS = pltpu.CompilerParams(vmem_limit_bytes=12 << 20)


def call(kernel, name, outs, scalars, arrays, scratch=(), out_specs=None):
    return pl.pallas_call(
        kernel,
        out_shape=tuple(jax.ShapeDtypeStruct(shape, dtype) for shape, dtype in outs),
        in_specs=[SMEM] * len(scalars) + [VMEM] * len(arrays),
        out_specs=tuple(out_specs or [VMEM] * len(outs)),
        scratch_shapes=[pltpu.VMEM(shape, F32) for shape in scratch],
        compiler_params=PARAMS,
        name=name,
    )(*scalars, *arrays)


def shards(estimate, view_data, psf_taps, offsets, coverage):
    depth, rows, width = estimate.shape
    views = view_data.shape[0]
    half = (psf_taps.shape[2] - 1) // 2
    reach = half + 1
    wide = rows + 2 * reach
    ring = lax.axis_size("brick")
    stacks = lax.axis_size("stack")
    up = [(i, i + 1) for i in range(stacks - 1)]
    down = [(i + 1, i) for i in range(stacks - 1)]
    right = [(i, i + 1) for i in range(ring - 1)]
    left = [(i + 1, i) for i in range(ring - 1)]

    parts = ring // depth
    strip = rows // parts
    spread_views = views - DIRECT
    order, moves, pieces, *straight = call(
        functools.partial(pick_kernel, ROW, ring // ROW),
        "pick",
        [((views,), jnp.int32)] * 2 + [((ring, spread_views, strip, width), F32)] + [((depth, rows, width), F32)] * DIRECT,
        [offsets],
        [view_data.reshape(views, ring, strip, width)],
        out_specs=[SMEM, SMEM] + [VMEM] * (1 + DIRECT),
    )
    head = lax.ppermute(estimate[:, rows - reach :], "brick", right)
    tail = lax.ppermute(estimate[:, :reach], "brick", left)
    pieces, head, tail = lax.optimization_barrier((pieces, head, tail))
    spread = lax.all_to_all(pieces, "brick", 0, 0, tiled=True)
    mid = jnp.concatenate([head, estimate, tail], axis=1)
    low = lax.ppermute(mid, "stack", up)
    high = lax.ppermute(mid, "stack", down)

    lateral_on, lateral_off, across_on, across_off = call(
        functools.partial(prepare_kernel, half, rows, wide),
        "prepare",
        [((views * rows, 3 * wide), BF16), ((2 * wide, views * rows), BF16)] + [((views, 2 * width, 2 * width), BF16)] * 2,
        [psf_taps],
        [],
    )

    hops = [lambda x: x]
    for by in range(1, ring):
        pairs = [(i, (i + by) % ring) for i in range(ring)]
        hops.append(functools.partial(lax.ppermute, axis_name="brick", perm=pairs))

    def send(slot, x):
        return lax.switch(moves[spread_views + slot], hops, x)

    sent = [send(slot, straight[slot]) for slot in range(EARLY)]
    spread, low, high, *sent = lax.optimization_barrier((spread, low, high, *sent))
    (turned,) = call(functools.partial(turn_kernel, ring), "turn", [(spread.shape, F32)], [moves], [spread])
    tiles = lax.all_to_all(turned, "brick", 0, 0, tiled=True)
    tiles = tiles.reshape(depth, parts, spread_views, strip, width)

    (blurred,) = call(
        functools.partial(forward_kernel, half),
        "forward",
        [((views, depth, rows, width), F32)],
        [psf_taps],
        [low, mid, high, lateral_on, across_on],
        [(3 * depth, views * rows, width)],
    )

    blurred, *waiting = lax.optimization_barrier((blurred, *straight[EARLY:]))
    sent += [send(EARLY + slot, x) for slot, x in enumerate(waiting)]

    slab = ((depth, wide, width), F32)
    near, below, above = call(
        functools.partial(outer_kernel, half),
        "outer",
        [((views, depth, rows, width), F32), slab, slab],
        [psf_taps, coverage[:, 0], order],
        [tiles, *sent, blurred, across_off, lateral_off],
        [(2 * depth, views * rows, width)],
    )
    from_above = lax.ppermute(below, "stack", down)
    from_below = lax.ppermute(above, "stack", up)
    (own,) = call(
        functools.partial(inner_kernel, half),
        "inner",
        [slab],
        [psf_taps],
        [near, lateral_off],
        [(depth, views * rows, width)],
    )

    def total(at):
        return own[:, at] + from_above[:, at] + from_below[:, at]

    faces = total(slice(0, reach)), total(slice(rows + reach, wide))
    from_right = lax.ppermute(faces[0], "brick", left)
    from_left = lax.ppermute(faces[1], "brick", right)
    summed = total(slice(reach, rows + reach))
    gap = jnp.zeros((depth, rows - reach, width), F32)
    summed = summed + jnp.concatenate([from_left, gap], axis=1) + jnp.concatenate([gap, from_right], axis=1)
    cover_count = jnp.sum(coverage[:, 0].astype(F32))
    return estimate * summed / cover_count


def solution(mesh):
    placed = (
        P("stack", "brick", None),
        P(None, "stack", "brick", None),
        P(),
        P(),
        P(None, "brick"),
    )
    return jax.shard_map(
        shards, mesh=mesh, in_specs=placed, out_specs=P("stack", "brick", None), check_vma=False
    )
```

```python
import functools

import jax
import jax.numpy as jnp
from jax import lax
from jax.experimental import pallas as pl
from jax.experimental.pallas import tpu as pltpu
from jax.sharding import PartitionSpec as P

F32, BF16 = jnp.float32, jnp.bfloat16
ROW = 8
DIRECT = 2
EARLY = 2


def split(values):
    high = values.astype(BF16)
    return high, (values - high.astype(F32)).astype(BF16)


def dot(left, right):
    return jnp.dot(left, right, preferred_element_type=F32)


def normal(taps_ref, view, dim):
    count = taps_ref.shape[2]
    total = taps_ref[view, dim, 0]
    for t in range(1, count):
        total = total + taps_ref[view, dim, t]
    scale = 1.0 / jnp.full((8, 128), total, F32)
    return [jnp.full((8, 128), taps_ref[view, dim, t], F32) * scale for t in range(count)]


def prepare_kernel(half, rows, wide, taps_ref, lateral_ref, lateral_back_ref, across_ref, across_back_ref):
    views, width = taps_ref.shape[0], 128

    def banded(taps, lane_of, count):
        lane = lax.broadcasted_iota(jnp.int32, (8, width), 1)
        first = jnp.zeros((8, width), F32)
        for t, tap in enumerate(taps):
            first = jnp.where(lane == lane_of(t) % width, tap, first)
        tall = jnp.concatenate([first] * (count // 8), axis=0)
        return pltpu.roll(tall, 0, 1, stride=1, stride_axis=0)

    row = lax.broadcasted_iota(jnp.int32, (width, width), 0)
    lane = lax.broadcasted_iota(jnp.int32, (width, width), 1)
    near = jnp.abs(row - lane) <= half
    back = [[jnp.zeros((wide, width), F32)] for _ in range(-(-views * rows // width))]
    for view in range(views):
        taps = normal(taps_ref, view, 2)
        for ref, lane_of in ((across_ref, lambda t: half - t), (across_back_ref, lambda t: t - half)):
            high, low = split(jnp.where(near, banded(taps, lane_of, width), 0.0))
            ref[view, :width, :width] = high
            ref[view, :width, width:] = low
            ref[view, width:, :width] = high
            ref[view, width:, width:] = jnp.zeros_like(low)
        taps = normal(taps_ref, view, 1)
        high, low = split(banded(taps, lambda t: t + 1, rows))
        high = high.astype(F32)
        at = slice(view * rows, (view + 1) * rows)
        lateral_ref[at, : 2 * wide] = (high + pltpu.roll(high, wide, 1)).astype(BF16)
        lateral_ref[at, 2 * wide :] = low[:, :wide]
        field = jnp.where(lane[:wide] < rows, banded(taps, lambda t: -1 - t, wide), 0.0)
        place = view * rows
        shift = place % width
        back[place // width].append(pltpu.roll(field, shift, 1) if shift else field)
    for block, fields in enumerate(back):
        total = fields[0]
        for field in fields[1:]:
            total = total + field
        high, low = split(total)
        size = min(width, views * rows - block * width)
        lateral_back_ref[:wide, block * width : block * width + size] = high[:, :size]
        lateral_back_ref[wide:, block * width : block * width + size] = low[:, :size]


def pair_of(ref, z):
    first_h, first_l = split(ref[z])
    second_h, second_l = split(ref[z + 1])
    return jnp.concatenate([first_h, second_h], axis=1), jnp.concatenate([first_l, second_l], axis=1)


def across_pass(field, matrix):
    depth, rows, width = field.shape
    upper, lower = split(field.reshape(depth * rows, width))
    both = dot(jnp.concatenate([upper, lower], axis=1), matrix)
    return (both[:, :width] + both[:, width:]).reshape(depth, rows, width)


def forward_kernel(half, taps_ref, low_ref, mid_ref, high_ref, lateral_ref, across_ref, out_ref, wide_ref):
    views, depth, rows, width = out_ref.shape
    for part, ref in enumerate((low_ref, mid_ref, high_ref)):

        def lateral(pair, carry, part=part, ref=ref):
            upper, lower = pair_of(ref, pair * 2)
            result = dot(lateral_ref[...], jnp.concatenate([upper, lower, upper], axis=0))
            wide_ref[part * depth + pair * 2] = result[:, :width]
            wide_ref[part * depth + pair * 2 + 1] = result[:, width:]
            return carry

        lax.fori_loop(0, depth // 2, lateral, 0, unroll=True)

    start, block = depth - half, 8

    def axial(view, carry):
        taps = normal(taps_ref, view, 0)
        for group in range(rows // 8):
            at = pl.ds(pl.multiple_of(view * rows + group * 8, 8), 8)
            for base in range(0, depth, block):
                totals = [None] * block
                for z in range(base, base + block + len(taps) - 1):
                    field = wide_ref[start + z, at, :]
                    for i in range(block):
                        t = z - base - i
                        if 0 <= t < len(taps):
                            term = taps[t] * field
                            totals[i] = term if totals[i] is None else totals[i] + term
                for i in range(block):
                    out_ref[view, base + i, group * 8 : group * 8 + 8, :] = totals[i]
        return carry

    lax.fori_loop(0, views, axial, 0)
    for view in range(views):
        out_ref[view] = across_pass(out_ref[view], across_ref[view])


def axial_back(half, taps_ref, near_ref, wide_ref, places, count, view_of, place_of):
    depth, rows, width = near_ref.shape[1:]
    start = depth - half

    def body(number, carry):
        taps, place = normal(taps_ref, view_of(number), 0), place_of(number)
        for group in range(rows // 8):
            into = pl.ds(pl.multiple_of(place * rows + group * 8, 8), 8)
            field = [near_ref[place, z, group * 8 : group * 8 + 8, :] for z in range(depth)]
            for slot, z in enumerate(places):
                total = None
                for source in range(depth):
                    t = z - start - source
                    if 0 <= t < len(taps):
                        term = taps[t] * field[source]
                        total = term if total is None else total + term
                wide_ref[slot, into, :] = jnp.zeros((8, width), F32) if total is None else total
        return carry

    lax.fori_loop(0, count, body, 0)


def lateral_back(lateral_ref, wide_ref, first, out_ref):
    depth, wide, width = out_ref.shape

    def body(pair, carry):
        upper, lower = pair_of(wide_ref, first + pair * 2)
        one = dot(lateral_ref[...], upper)
        result = one[:wide] + one[wide:] + dot(lateral_ref[:wide], lower)
        out_ref[pair * 2] = result[:, :width]
        out_ref[pair * 2 + 1] = result[:, width:]
        return carry

    lax.fori_loop(0, depth // 2, body, 0, unroll=True)


def outer_places(depth):
    return list(range(depth)) + list(range(2 * depth, 3 * depth))


def ahead_kernel(half, taps_ref, cover_ref, order_ref, *refs):
    *direct, blurred_ref, across_ref, near_ref, wide_ref = refs
    depth = blurred_ref.shape[1]
    first = blurred_ref.shape[0] - len(direct)
    for number, tile_ref in enumerate(direct):
        view = order_ref[first + number]
        near_ref[number] = across_pass(cover_ref[view].astype(F32) * tile_ref[...] / blurred_ref[view], across_ref[view])
    view_of = lambda number: order_ref[first + number]
    axial_back(half, taps_ref, near_ref, wide_ref, outer_places(depth), len(direct), view_of, lambda number: number)


def outer_kernel(half, taps_ref, cover_ref, order_ref, *refs):
    tiles_ref, near_ahead_ref, wide_ahead_ref, blurred_ref, across_ref, lateral_ref, near_ref, low_ref, high_ref, wide_ref = refs
    views, depth, rows, width = blurred_ref.shape
    halves, spread = tiles_ref.shape[1:3]
    for slot in range(views):
        view = order_ref[slot]
        if slot < spread:
            owned = jnp.concatenate([tiles_ref[:, part, slot] for part in range(halves)], axis=1)
            ratio = cover_ref[view].astype(F32) * owned / blurred_ref[view]
            near_ref[view] = across_pass(ratio, across_ref[view])
        else:
            number = slot - spread
            near_ref[view] = near_ahead_ref[number]
            at = pl.ds(pl.multiple_of(view * rows, 8), rows)
            wide_ref[:, at, :] = wide_ahead_ref[:, number * rows : (number + 1) * rows, :]
    view_of = lambda slot: order_ref[slot]
    axial_back(half, taps_ref, near_ref, wide_ref, outer_places(depth), spread, view_of, view_of)
    lateral_back(lateral_ref, wide_ref, 0, low_ref)
    lateral_back(lateral_ref, wide_ref, depth, high_ref)


def inner_kernel(half, taps_ref, near_ref, lateral_ref, mid_ref, wide_ref):
    views, depth = near_ref.shape[:2]
    same = lambda view: view
    axial_back(half, taps_ref, near_ref, wide_ref, list(range(depth, 2 * depth)), views, same, same)
    lateral_back(lateral_ref, wide_ref, 0, mid_ref)


def turn_kernel(ring, offsets_ref, in_ref, out_ref):
    views = in_ref.shape[1]

    def body(place, carry):
        for view in range(views):
            source = lax.rem(place + ring - offsets_ref[view], ring)
            out_ref[place, view] = in_ref[source, view]
        return carry

    lax.fori_loop(0, ring, body, 0)


def pick_kernel(row, columns, offsets_ref, in_ref, order_ref, sorted_ref, pieces_ref, *direct):
    views = in_ref.shape[0]
    spread = pieces_ref.shape[1]
    cost, moves = [], []
    for view in range(views):
        move = lax.rem(offsets_ref[view], row * columns)
        across, along = lax.rem(move, row), move // row
        near = 2 * jnp.minimum(along, columns - along)
        far = 2 * jnp.minimum(along + 1, columns - 1 - along)
        far = jnp.where(across > 0, far, 0)
        cost.append(jnp.maximum(jnp.minimum(across, row - across), jnp.maximum(near, far)))
        moves.append(move)
    for view in range(views):
        rank = jnp.int32(0)
        for other in range(views):
            if other != view:
                ahead = cost[other] >= cost[view] if other < view else cost[other] > cost[view]
                rank = rank + ahead.astype(jnp.int32)
        order_ref[rank] = jnp.int32(view)
        sorted_ref[rank] = moves[view]
    for slot in range(views):
        view = order_ref[slot]
        if slot < spread:
            pieces_ref[:, slot] = in_ref[view]
        else:
            direct[slot - spread][...] = in_ref[view].reshape(direct[slot - spread].shape)


SMEM = pl.BlockSpec(memory_space=pltpu.SMEM)
VMEM = pl.BlockSpec(memory_space=pltpu.VMEM)
PARAMS = pltpu.CompilerParams(vmem_limit_bytes=12 << 20)


def call(kernel, name, outs, scalars, arrays, scratch=(), out_specs=None):
    return pl.pallas_call(
        kernel,
        out_shape=tuple(jax.ShapeDtypeStruct(shape, dtype) for shape, dtype in outs),
        in_specs=[SMEM] * len(scalars) + [VMEM] * len(arrays),
        out_specs=tuple(out_specs or [VMEM] * len(outs)),
        scratch_shapes=[pltpu.VMEM(shape, F32) for shape in scratch],
        compiler_params=PARAMS,
        name=name,
    )(*scalars, *arrays)


def shards(estimate, view_data, psf_taps, offsets, coverage):
    depth, rows, width = estimate.shape
    views = view_data.shape[0]
    half = (psf_taps.shape[2] - 1) // 2
    reach = half + 1
    wide = rows + 2 * reach
    ring = lax.axis_size("brick")
    stacks = lax.axis_size("stack")
    up = [(i, i + 1) for i in range(stacks - 1)]
    down = [(i + 1, i) for i in range(stacks - 1)]
    right = [(i, i + 1) for i in range(ring - 1)]
    left = [(i + 1, i) for i in range(ring - 1)]

    parts = ring // depth
    strip = rows // parts
    spread_views = views - DIRECT
    order, moves, pieces, *straight = call(
        functools.partial(pick_kernel, ROW, ring // ROW),
        "pick",
        [((views,), jnp.int32)] * 2 + [((ring, spread_views, strip, width), F32)] + [((depth, rows, width), F32)] * DIRECT,
        [offsets],
        [view_data.reshape(views, ring, strip, width)],
        out_specs=[SMEM, SMEM] + [VMEM] * (1 + DIRECT),
    )
    head = lax.ppermute(estimate[:, rows - reach :], "brick", right)
    tail = lax.ppermute(estimate[:, :reach], "brick", left)
    pieces, head, tail = lax.optimization_barrier((pieces, head, tail))
    spread = lax.all_to_all(pieces, "brick", 0, 0, tiled=True)
    mid = jnp.concatenate([head, estimate, tail], axis=1)
    low = lax.ppermute(mid, "stack", up)
    high = lax.ppermute(mid, "stack", down)

    lateral_on, lateral_off, across_on, across_off = call(
        functools.partial(prepare_kernel, half, rows, wide),
        "prepare",
        [((views * rows, 3 * wide), BF16), ((2 * wide, views * rows), BF16)] + [((views, 2 * width, 2 * width), BF16)] * 2,
        [psf_taps],
        [],
    )

    hops = [lambda x: x]
    for by in range(1, ring):
        pairs = [(i, (i + by) % ring) for i in range(ring)]
        hops.append(functools.partial(lax.ppermute, axis_name="brick", perm=pairs))

    def send(slot, x):
        return lax.switch(moves[spread_views + slot], hops, x)

    sent = [send(slot, straight[slot]) for slot in range(EARLY)]
    spread, low, high, *sent = lax.optimization_barrier((spread, low, high, *sent))
    (turned,) = call(functools.partial(turn_kernel, ring), "turn", [(spread.shape, F32)], [moves], [spread])
    tiles = lax.all_to_all(turned, "brick", 0, 0, tiled=True)
    tiles = tiles.reshape(depth, parts, spread_views, strip, width)

    (blurred,) = call(
        functools.partial(forward_kernel, half),
        "forward",
        [((views, depth, rows, width), F32)],
        [psf_taps],
        [low, mid, high, lateral_on, across_on],
        [(3 * depth, views * rows, width)],
    )

    blurred, *waiting = lax.optimization_barrier((blurred, *straight[EARLY:]))
    sent += [send(EARLY + slot, x) for slot, x in enumerate(waiting)]

    near_ahead, wide_ahead = call(
        functools.partial(ahead_kernel, half),
        "ahead",
        [((DIRECT, depth, rows, width), F32), ((2 * depth, DIRECT * rows, width), F32)],
        [psf_taps, coverage[:, 0], order],
        [*sent, blurred, across_off],
    )
    slab = ((depth, wide, width), F32)
    near, below, above = call(
        functools.partial(outer_kernel, half),
        "outer",
        [((views, depth, rows, width), F32), slab, slab],
        [psf_taps, coverage[:, 0], order],
        [tiles, near_ahead, wide_ahead, blurred, across_off, lateral_off],
        [(2 * depth, views * rows, width)],
    )
    from_above = lax.ppermute(below, "stack", down)
    from_below = lax.ppermute(above, "stack", up)
    (own,) = call(
        functools.partial(inner_kernel, half),
        "inner",
        [slab],
        [psf_taps],
        [near, lateral_off],
        [(depth, views * rows, width)],
    )

    def total(at):
        return own[:, at] + from_above[:, at] + from_below[:, at]

    faces = total(slice(0, reach)), total(slice(rows + reach, wide))
    from_right = lax.ppermute(faces[0], "brick", left)
    from_left = lax.ppermute(faces[1], "brick", right)
    summed = total(slice(reach, rows + reach))
    gap = jnp.zeros((depth, rows - reach, width), F32)
    summed = summed + jnp.concatenate([from_left, gap], axis=1) + jnp.concatenate([gap, from_right], axis=1)
    cover_count = jnp.sum(coverage[:, 0].astype(F32))
    return estimate * summed / cover_count


def solution(mesh):
    placed = (
        P("stack", "brick", None),
        P(None, "stack", "brick", None),
        P(),
        P(),
        P(None, "brick"),
    )
    return jax.shard_map(
        shards, mesh=mesh, in_specs=placed, out_specs=P("stack", "brick", None), check_vma=False
    )
```

```python
import functools

import jax
import jax.numpy as jnp
from jax import lax
from jax.experimental import pallas as pl
from jax.experimental.pallas import tpu as pltpu
from jax.sharding import PartitionSpec as P

F32, BF16 = jnp.float32, jnp.bfloat16
ROW = 8
DIRECT = 2
EARLY = 1


def split(values):
    high = values.astype(BF16)
    return high, (values - high.astype(F32)).astype(BF16)


def dot(left, right):
    return jnp.dot(left, right, preferred_element_type=F32)


def normal(taps_ref, view, dim):
    count = taps_ref.shape[2]
    total = taps_ref[view, dim, 0]
    for t in range(1, count):
        total = total + taps_ref[view, dim, t]
    scale = 1.0 / jnp.full((8, 128), total, F32)
    return [jnp.full((8, 128), taps_ref[view, dim, t], F32) * scale for t in range(count)]


def prepare_kernel(half, rows, wide, taps_ref, lateral_ref, lateral_back_ref, across_ref, across_back_ref):
    views, width = taps_ref.shape[0], 128

    def banded(taps, lane_of, count):
        lane = lax.broadcasted_iota(jnp.int32, (8, width), 1)
        first = jnp.zeros((8, width), F32)
        for t, tap in enumerate(taps):
            first = jnp.where(lane == lane_of(t) % width, tap, first)
        tall = jnp.concatenate([first] * (count // 8), axis=0)
        return pltpu.roll(tall, 0, 1, stride=1, stride_axis=0)

    row = lax.broadcasted_iota(jnp.int32, (width, width), 0)
    lane = lax.broadcasted_iota(jnp.int32, (width, width), 1)
    near = jnp.abs(row - lane) <= half
    back = [[jnp.zeros((wide, width), F32)] for _ in range(-(-views * rows // width))]
    for view in range(views):
        taps = normal(taps_ref, view, 2)
        for ref, lane_of in ((across_ref, lambda t: half - t), (across_back_ref, lambda t: t - half)):
            high, low = split(jnp.where(near, banded(taps, lane_of, width), 0.0))
            ref[view, :width, :width] = high
            ref[view, :width, width:] = low
            ref[view, width:, :width] = high
            ref[view, width:, width:] = jnp.zeros_like(low)
        taps = normal(taps_ref, view, 1)
        high, low = split(banded(taps, lambda t: t + 1, rows))
        high = high.astype(F32)
        at = slice(view * rows, (view + 1) * rows)
        lateral_ref[at, : 2 * wide] = (high + pltpu.roll(high, wide, 1)).astype(BF16)
        lateral_ref[at, 2 * wide :] = low[:, :wide]
        field = jnp.where(lane[:wide] < rows, banded(taps, lambda t: -1 - t, wide), 0.0)
        place = view * rows
        shift = place % width
        back[place // width].append(pltpu.roll(field, shift, 1) if shift else field)
    for block, fields in enumerate(back):
        total = fields[0]
        for field in fields[1:]:
            total = total + field
        high, low = split(total)
        size = min(width, views * rows - block * width)
        lateral_back_ref[:wide, block * width : block * width + size] = high[:, :size]
        lateral_back_ref[wide:, block * width : block * width + size] = low[:, :size]


def pair_of(ref, z):
    first_h, first_l = split(ref[z])
    second_h, second_l = split(ref[z + 1])
    return jnp.concatenate([first_h, second_h], axis=1), jnp.concatenate([first_l, second_l], axis=1)


def across_pass(field, matrix):
    depth, rows, width = field.shape
    upper, lower = split(field.reshape(depth * rows, width))
    both = dot(jnp.concatenate([upper, lower], axis=1), matrix)
    return (both[:, :width] + both[:, width:]).reshape(depth, rows, width)


def forward_kernel(half, taps_ref, low_ref, mid_ref, high_ref, lateral_ref, across_ref, out_ref, wide_ref):
    views, depth, rows, width = out_ref.shape
    for part, ref in enumerate((low_ref, mid_ref, high_ref)):

        def lateral(pair, carry, part=part, ref=ref):
            upper, lower = pair_of(ref, pair * 2)
            result = dot(lateral_ref[...], jnp.concatenate([upper, lower, upper], axis=0))
            wide_ref[part * depth + pair * 2] = result[:, :width]
            wide_ref[part * depth + pair * 2 + 1] = result[:, width:]
            return carry

        lax.fori_loop(0, depth // 2, lateral, 0, unroll=True)

    start, block = depth - half, 8

    def axial(view, carry):
        taps = normal(taps_ref, view, 0)
        for group in range(rows // 8):
            at = pl.ds(pl.multiple_of(view * rows + group * 8, 8), 8)
            for base in range(0, depth, block):
                totals = [None] * block
                for z in range(base, base + block + len(taps) - 1):
                    field = wide_ref[start + z, at, :]
                    for i in range(block):
                        t = z - base - i
                        if 0 <= t < len(taps):
                            term = taps[t] * field
                            totals[i] = term if totals[i] is None else totals[i] + term
                for i in range(block):
                    out_ref[view, base + i, group * 8 : group * 8 + 8, :] = totals[i]
        return carry

    lax.fori_loop(0, views, axial, 0)
    for view in range(views):
        out_ref[view] = across_pass(out_ref[view], across_ref[view])


def axial_back(half, taps_ref, near_ref, wide_ref, places):
    views, depth, rows, width = near_ref.shape
    start = depth - half

    def body(view, carry):
        taps = normal(taps_ref, view, 0)
        for group in range(rows // 8):
            into = pl.ds(pl.multiple_of(view * rows + group * 8, 8), 8)
            field = [near_ref[view, z, group * 8 : group * 8 + 8, :] for z in range(depth)]
            for slot, z in enumerate(places):
                total = None
                for source in range(depth):
                    t = z - start - source
                    if 0 <= t < len(taps):
                        term = taps[t] * field[source]
                        total = term if total is None else total + term
                wide_ref[slot, into, :] = jnp.zeros((8, width), F32) if total is None else total
        return carry

    lax.fori_loop(0, views, body, 0)


def lateral_back(lateral_ref, wide_ref, first, out_ref):
    depth, wide, width = out_ref.shape

    def body(pair, carry):
        upper, lower = pair_of(wide_ref, first + pair * 2)
        one = dot(lateral_ref[...], upper)
        result = one[:wide] + one[wide:] + dot(lateral_ref[:wide], lower)
        out_ref[pair * 2] = result[:, :width]
        out_ref[pair * 2 + 1] = result[:, width:]
        return carry

    lax.fori_loop(0, depth // 2, body, 0, unroll=True)


def outer_kernel(half, taps_ref, cover_ref, order_ref, *refs):
    tiles_ref, *direct = refs[:-7]
    blurred_ref, across_ref, lateral_ref, near_ref, low_ref, high_ref, wide_ref = refs[-7:]
    views, depth, rows, width = blurred_ref.shape
    halves, spread = tiles_ref.shape[1:3]
    for slot in range(views):
        view = order_ref[slot]
        if slot < spread:
            owned = jnp.concatenate([tiles_ref[:, part, slot] for part in range(halves)], axis=1)
        else:
            owned = direct[slot - spread][...]
        ratio = cover_ref[view].astype(F32) * owned / blurred_ref[view]
        near_ref[view] = across_pass(ratio, across_ref[view])
    axial_back(half, taps_ref, near_ref, wide_ref, list(range(depth)) + list(range(2 * depth, 3 * depth)))
    lateral_back(lateral_ref, wide_ref, 0, low_ref)
    lateral_back(lateral_ref, wide_ref, depth, high_ref)


def inner_kernel(half, taps_ref, near_ref, lateral_ref, mid_ref, wide_ref):
    depth = near_ref.shape[1]
    axial_back(half, taps_ref, near_ref, wide_ref, list(range(depth, 2 * depth)))
    lateral_back(lateral_ref, wide_ref, 0, mid_ref)


def turn_kernel(ring, offsets_ref, in_ref, out_ref):
    views = in_ref.shape[1]

    def body(place, carry):
        for view in range(views):
            source = lax.rem(place + ring - offsets_ref[view], ring)
            out_ref[place, view] = in_ref[source, view]
        return carry

    lax.fori_loop(0, ring, body, 0)


def pick_kernel(row, columns, offsets_ref, in_ref, order_ref, sorted_ref, pieces_ref, *direct):
    views = in_ref.shape[0]
    spread = pieces_ref.shape[1]
    cost, moves = [], []
    for view in range(views):
        move = lax.rem(offsets_ref[view], row * columns)
        across, along = lax.rem(move, row), move // row
        near = 2 * jnp.minimum(along, columns - along)
        far = 2 * jnp.minimum(along + 1, columns - 1 - along)
        far = jnp.where(across > 0, far, 0)
        cost.append(jnp.maximum(jnp.minimum(across, row - across), jnp.maximum(near, far)))
        moves.append(move)
    for view in range(views):
        rank = jnp.int32(0)
        for other in range(views):
            if other != view:
                ahead = cost[other] >= cost[view] if other < view else cost[other] > cost[view]
                rank = rank + ahead.astype(jnp.int32)
        order_ref[rank] = jnp.int32(view)
        sorted_ref[rank] = moves[view]
    for slot in range(views):
        view = order_ref[slot]
        if slot < spread:
            pieces_ref[:, slot] = in_ref[view]
        else:
            direct[slot - spread][...] = in_ref[view].reshape(direct[slot - spread].shape)


SMEM = pl.BlockSpec(memory_space=pltpu.SMEM)
VMEM = pl.BlockSpec(memory_space=pltpu.VMEM)
PARAMS = pltpu.CompilerParams(vmem_limit_bytes=12 << 20)


def call(kernel, name, outs, scalars, arrays, scratch=(), out_specs=None):
    return pl.pallas_call(
        kernel,
        out_shape=tuple(jax.ShapeDtypeStruct(shape, dtype) for shape, dtype in outs),
        in_specs=[SMEM] * len(scalars) + [VMEM] * len(arrays),
        out_specs=tuple(out_specs or [VMEM] * len(outs)),
        scratch_shapes=[pltpu.VMEM(shape, F32) for shape in scratch],
        compiler_params=PARAMS,
        name=name,
    )(*scalars, *arrays)


def shards(estimate, view_data, psf_taps, offsets, coverage):
    depth, rows, width = estimate.shape
    views = view_data.shape[0]
    half = (psf_taps.shape[2] - 1) // 2
    reach = half + 1
    wide = rows + 2 * reach
    ring = lax.axis_size("brick")
    stacks = lax.axis_size("stack")
    up = [(i, i + 1) for i in range(stacks - 1)]
    down = [(i + 1, i) for i in range(stacks - 1)]
    right = [(i, i + 1) for i in range(ring - 1)]
    left = [(i + 1, i) for i in range(ring - 1)]

    parts = ring // depth
    strip = rows // parts
    spread_views = views - DIRECT
    order, moves, pieces, *straight = call(
        functools.partial(pick_kernel, ROW, ring // ROW),
        "pick",
        [((views,), jnp.int32)] * 2 + [((ring, spread_views, strip, width), F32)] + [((depth, rows, width), F32)] * DIRECT,
        [offsets],
        [view_data.reshape(views, ring, strip, width)],
        out_specs=[SMEM, SMEM] + [VMEM] * (1 + DIRECT),
    )
    head = lax.ppermute(estimate[:, rows - reach :], "brick", right)
    tail = lax.ppermute(estimate[:, :reach], "brick", left)
    pieces, head, tail = lax.optimization_barrier((pieces, head, tail))
    spread = lax.all_to_all(pieces, "brick", 0, 0, tiled=True)
    mid = jnp.concatenate([head, estimate, tail], axis=1)
    low = lax.ppermute(mid, "stack", up)
    high = lax.ppermute(mid, "stack", down)

    lateral_on, lateral_off, across_on, across_off = call(
        functools.partial(prepare_kernel, half, rows, wide),
        "prepare",
        [((views * rows, 3 * wide), BF16), ((2 * wide, views * rows), BF16)] + [((views, 2 * width, 2 * width), BF16)] * 2,
        [psf_taps],
        [],
    )

    hops = [lambda x: x]
    for by in range(1, ring):
        pairs = [(i, (i + by) % ring) for i in range(ring)]
        hops.append(functools.partial(lax.ppermute, axis_name="brick", perm=pairs))

    def send(slot, x):
        return lax.switch(moves[spread_views + slot], hops, x)

    sent = [send(slot, straight[slot]) for slot in range(EARLY)]
    spread, low, high, *sent = lax.optimization_barrier((spread, low, high, *sent))
    (turned,) = call(functools.partial(turn_kernel, ring), "turn", [(spread.shape, F32)], [moves], [spread])
    tiles = lax.all_to_all(turned, "brick", 0, 0, tiled=True)
    tiles = tiles.reshape(depth, parts, spread_views, strip, width)

    (blurred,) = call(
        functools.partial(forward_kernel, half),
        "forward",
        [((views, depth, rows, width), F32)],
        [psf_taps],
        [low, mid, high, lateral_on, across_on],
        [(3 * depth, views * rows, width)],
    )

    blurred, *waiting = lax.optimization_barrier((blurred, *straight[EARLY:]))
    sent += [send(EARLY + slot, x) for slot, x in enumerate(waiting)]

    slab = ((depth, wide, width), F32)
    near, below, above = call(
        functools.partial(outer_kernel, half),
        "outer",
        [((views, depth, rows, width), F32), slab, slab],
        [psf_taps, coverage[:, 0], order],
        [tiles, *sent, blurred, across_off, lateral_off],
        [(2 * depth, views * rows, width)],
    )
    from_above = lax.ppermute(below, "stack", down)
    from_below = lax.ppermute(above, "stack", up)
    (own,) = call(
        functools.partial(inner_kernel, half),
        "inner",
        [slab],
        [psf_taps],
        [near, lateral_off],
        [(depth, views * rows, width)],
    )

    def total(at):
        return own[:, at] + from_above[:, at] + from_below[:, at]

    faces = total(slice(0, reach)), total(slice(rows + reach, wide))
    from_right = lax.ppermute(faces[0], "brick", left)
    from_left = lax.ppermute(faces[1], "brick", right)
    summed = total(slice(reach, rows + reach))
    gap = jnp.zeros((depth, rows - reach, width), F32)
    summed = summed + jnp.concatenate([from_left, gap], axis=1) + jnp.concatenate([gap, from_right], axis=1)
    cover_count = jnp.sum(coverage[:, 0].astype(F32))
    return estimate * summed / cover_count


def solution(mesh):
    placed = (
        P("stack", "brick", None),
        P(None, "stack", "brick", None),
        P(),
        P(),
        P(None, "brick"),
    )
    return jax.shard_map(
        shards, mesh=mesh, in_specs=placed, out_specs=P("stack", "brick", None), check_vma=False
    )
```
